32 devices in a mesh: samp: 8 (over y, x, core), exp: 4 (over z).
Axes of the slice: x: 2, y: 2, z: 4, core: 2. Of those that a mesh axis runs over, the one named last changes fastest.
Arguments:
- prompt_states: bfloat16 [4, 8, 64, 2048], P('exp', 'samp'), may hold values from -6 to 6
- edit_offsets: bfloat16 [1, 4, 8, 64, 2048], P(None, 'exp', 'samp'), may hold values from -6 to 6
- targets: bfloat16 [2, 4, 8, 64, 2048], P(None, 'exp', 'samp'), may hold values from -6 to 6
- router: bfloat16 [2048, 32], replicated, may hold values from -0.125 to 0.125
- route_ids: int32 [2, 4, 8, 64, 8], P(None, 'exp', 'samp'), may hold values from 0 to 31, all different within a row; in each aligned block of 64 rows (0 to 63, 64 to 127, ..., all dimensions but the last counted through in order) at most 20 rows name the same one
- chosen: int32 [1, 4], replicated, may hold values from 0 to 7
- lengths: int32 [2, 4, 8], P(None, 'exp', 'samp'), may hold values from 16 to 64, as said below
- w_gate: bfloat16 [32, 2048, 768], P(('samp', 'exp')), may hold values from -0.125 to 0.125
- w_up: bfloat16 [32, 2048, 768], P(('samp', 'exp')), may hold values from -0.125 to 0.125
- w_down: bfloat16 [32, 768, 2048], P(('samp', 'exp')), may hold values from -0.21875 to 0.21875
Outputs:
- grad_gate: bfloat16 [32, 2048, 768], P(('samp', 'exp'))
- grad_up: bfloat16 [32, 2048, 768], P(('samp', 'exp'))
- grad_down: bfloat16 [32, 768, 2048], P(('samp', 'exp'))
- advantages: float32 [2, 4, 8], P(None, 'exp', 'samp')
The draws below stay inside these ranges and needn't reach their ends.
Inputs may be any that keep to these rules, and one draw needn't show every extreme that they name: `route_ids`: in each block of 64 rows that one repair has in one round, the 8 ids of a row differ, no expert is named by more than 20 rows, a bound that some block reaches. `lengths`: in each round and prompt some sample has exactly 64 scored tokens.
All inputs are finite; a program needn't handle non-finite values.
Results may differ from the reference program's by a relative error of at most 0.015.
Values may be sent and summed in bfloat16 or wider, within the bound.
A program may use at most 128 MiB of HBM per device.

```python
import math
import jax
import jax.numpy as jnp
import numpy as np
from jax import lax

D = 2048
FF = 768
TOP = 8
SEQ = 64
ROUNDS = 2
SAMPLES = 8
GROUPS = 4
EXPERTS = 32
CAP = 20


def draw_lengths(key, part):
    first_key, second_key = jax.random.split(jax.random.fold_in(key, 11))
    drawn = jax.random.randint(first_key, (ROUNDS, GROUPS, SAMPLES), SEQ // 4, SEQ + 1)
    longest = jax.random.randint(second_key, (ROUNDS, GROUPS, 1), 0, SAMPLES)
    sample_iota = jnp.arange(SAMPLES, dtype=jnp.int32)[None, None, :]
    return jnp.where(sample_iota == longest, SEQ, drawn).astype(jnp.int32)


def place_ends(values, key, low, largest):
    place = [jax.random.randint(jax.random.fold_in(key, axis), (), 0, length) for axis, length in enumerate(values.shape)]
    widest = values.shape.index(max(values.shape))
    neighbour = place[:widest] + [(place[widest] + 1) % values.shape[widest]] + place[widest + 1:]
    return values.at[tuple(place)].set(low).at[tuple(neighbour)].set(largest)


def block_levels(rng, dims, cuts, low, top_value):
    def one(dim, shards_of):
        steps = jax.random.uniform(jax.random.fold_in(jax.random.fold_in(rng, 6), dim), (shards_of,), jnp.float32, low / len(cuts), top_value / len(cuts))
        return jnp.repeat(jnp.exp(steps), dims[dim] // shards_of).reshape((-1,) + (1,) * (len(dims) - dim - 1))

    gain = one(*cuts[0])
    for cut in cuts[1:]:
        gain = gain * one(*cut)
    return gain


def routed_block(stream_key, own, number, rows, amount, top, reach, skew):
    order = jax.random.permutation(stream_key, amount)
    crowded, ordinary = load_shares(amount, rows * top, reach, skew, True), load_shares(amount, rows * top, reach, skew, False)
    places = jnp.arange(amount)

    def named(sizes, rotation):
        used = int((sizes > 0).sum())
        fixed = max(1, used // 4)
        moved = fixed + (places - fixed + rotation * (used - fixed)) % max(1, amount - fixed)
        return jnp.zeros((amount,), jnp.int32).at[order[jnp.where(places < fixed, places, moved)]].set(jnp.asarray(sizes, jnp.int32))

    sizes = jnp.where(number % 4 == 0, named(crowded, number // 4), named(ordinary, number - number // 4 - 1))
    mixed = jax.random.permutation(jax.random.fold_in(own, 3), amount)
    source_of, receiver = mixed[0:amount // 2 * 2:2], mixed[1:amount // 2 * 2:2]
    room = jnp.minimum(sizes[source_of] - 1, reach - sizes[receiver]) // 2
    room = jnp.where((source_of == order[0]) | (receiver == order[0]) | (sizes[receiver] == 0), 0, jnp.maximum(room, 0))
    moved = jax.random.randint(jax.random.fold_in(own, 4), (amount // 2,), 0, 1 << 20) % (room + 1)
    sizes = sizes.at[source_of].add(-moved).at[receiver].add(moved)
    items = jnp.searchsorted(jnp.cumsum(sizes), jnp.arange(rows * top), side="right").astype(jnp.int32)
    grid = items.reshape(top, rows).T
    grid = grid[jax.random.permutation(jax.random.fold_in(own, 1), rows)]
    rotation = jax.random.randint(jax.random.fold_in(own, 2), (rows, 1), 0, top)
    return jnp.take_along_axis(grid, (jnp.arange(top)[None, :] + rotation) % top, axis=1)


def load_shares(amount, total, limit, skew, full):
    loads = [(1 << 20) // math.isqrt(grade ** skew) + 1 for grade in range(1, amount + 1)]
    largest = limit if full else min(limit, max(-(-total // amount), total * loads[0] // sum(loads)))
    least = 1 if total - largest >= amount - 1 else 0
    counts, surplus = [largest] + [least] * (amount - 1), total - largest - least * (amount - 1)
    while surplus > 0:
        candidates = [i for i in range(1, amount) if counts[i] < largest] or [i for i in range(1, amount) if counts[i] < limit]
        mass, left = sum([loads[i] for i in candidates]), surplus
        for i in candidates:
            extra = min(limit - counts[i], max(1, left * loads[i] // mass), surplus)
            counts[i] = counts[i] + extra
            surplus = surplus - extra
    return np.array(counts)


def bell_draw(key, extent, deviation, limit, pieces=(), kind=jnp.bfloat16):
    loudness = block_levels(key, extent, pieces, -0.22, 0.18) if pieces else 1.0
    array = jax.random.normal(key, extent, jnp.float32) * deviation * loudness
    return jnp.minimum(jnp.maximum(array, -limit), limit).astype(kind)


def setup_inputs(seed: int = 0) -> dict:
    streams_of = jax.random.split(jax.random.key(seed), 11)
    prompt_states = bell_draw(streams_of[0], (GROUPS, SAMPLES, SEQ, D), 1.0, 6.0, ((0, 4), (1, 8)))
    edit_offsets = bell_draw(streams_of[1], (ROUNDS - 1, GROUPS, SAMPLES, SEQ, D), 1.0, 6.0, ((1, 4), (2, 8)))
    targets = bell_draw(streams_of[2], (ROUNDS, GROUPS, SAMPLES, SEQ, D), 1.0, 6.0, ((1, 4), (2, 8)))
    router = bell_draw(streams_of[3], (D, EXPERTS), D ** -0.5, 0.125)
    route_ids_keys = jax.random.split(jax.random.fold_in(streams_of[4], 1), ROUNDS * GROUPS * SAMPLES * SEQ // SEQ)
    route_ids_turns = jax.random.permutation(jax.random.fold_in(streams_of[4], 3), ROUNDS * GROUPS * SAMPLES * SEQ // SEQ)
    route_ids = jax.vmap(lambda own, number: routed_block(jax.random.fold_in(streams_of[4], 2), own, number, SEQ, EXPERTS, TOP, CAP, 1))(route_ids_keys, route_ids_turns).reshape((ROUNDS, GROUPS, SAMPLES, SEQ, TOP))
    chosen = place_ends(jax.random.randint(streams_of[5], (ROUNDS - 1, GROUPS), 0, SAMPLES), jax.random.fold_in(streams_of[5], 1), 0, SAMPLES - 1).astype(jnp.int32)
    lengths = draw_lengths(jax.random.fold_in(streams_of[10], 71), 0)
    w_gate = bell_draw(streams_of[7], (EXPERTS, D, FF), D ** -0.5, 0.125, ((0, 32),))
    w_up = bell_draw(streams_of[8], (EXPERTS, D, FF), D ** -0.5, 0.125, ((0, 32),))
    w_down = bell_draw(streams_of[9], (EXPERTS, FF, D), FF ** -0.5, 0.21875, ((0, 32),))
    return {"prompt_states": prompt_states, "edit_offsets": edit_offsets, "targets": targets, "router": router, "route_ids": route_ids, "chosen": chosen, "lengths": lengths, "w_gate": w_gate, "w_up": w_up, "w_down": w_down}


def expert_pass(expert_rows, gate_weight, up_weight, down_weight):
    pre_gate = jnp.dot(expert_rows, gate_weight, preferred_element_type=jnp.float32)
    pre_up = jnp.dot(expert_rows, up_weight, preferred_element_type=jnp.float32)
    hidden = (jax.nn.silu(pre_gate) * pre_up).astype(jnp.bfloat16)
    result = jnp.dot(hidden, down_weight, preferred_element_type=jnp.float32).astype(jnp.bfloat16)
    return (pre_gate, pre_up, hidden, result)

def build_table(route_now):
    flat_ids = route_now.reshape(GROUPS, SAMPLES, SEQ * TOP)
    onehot = (flat_ids[..., None] == jnp.arange(EXPERTS, dtype=jnp.int32)).astype(jnp.int32)
    slot_index = lax.optimization_barrier(jnp.sum(jnp.cumsum(onehot, axis=2) * onehot, axis=3)) - 1
    source = jnp.arange(SAMPLES, dtype=jnp.int32)[None, :, None] * GROUPS + jnp.arange(GROUPS, dtype=jnp.int32)[:, None, None]
    position = (source * CAP + slot_index).astype(jnp.int32)
    pair_index = jnp.arange(GROUPS * SAMPLES * SEQ * TOP, dtype=jnp.int32).reshape(GROUPS, SAMPLES, SEQ * TOP)
    empty_pair = GROUPS * SAMPLES * SEQ * TOP
    pair_table = jnp.full((EXPERTS, GROUPS * SAMPLES * CAP), empty_pair, dtype=jnp.int32)
    return pair_table.at[flat_ids, position].set(pair_index)

def padded(values, width_tail):
    return jnp.concatenate([values, jnp.zeros((1,) + width_tail, values.dtype)], axis=0)

def forward_round(tokens_now, route_now, router, w_gate, w_up, w_down):
    token_count = GROUPS * SAMPLES * SEQ
    token_flat = tokens_now.reshape(token_count, D)
    logits = jnp.dot(token_flat, router, preferred_element_type=jnp.float32).reshape(GROUPS, SAMPLES, SEQ, EXPERTS)
    picked = jnp.take_along_axis(logits, route_now, axis=3)
    sigmoid_values = jax.nn.sigmoid(picked)
    gate_values = (sigmoid_values / lax.optimization_barrier(jnp.sum(sigmoid_values, axis=3, keepdims=True))).astype(jnp.bfloat16)
    pair_table = build_table(route_now)
    token_pad = padded(token_flat, (D,))
    gate_pad = padded(gate_values.reshape(token_count * TOP).astype(jnp.float32), ())

    def step_fn(summed, inputs):
        pair_ids, gate_weight, up_weight, down_weight = inputs
        row_ids = pair_ids // TOP
        unused_a, unused_b, unused_c, result = expert_pass(token_pad[row_ids], gate_weight, up_weight, down_weight)
        return (summed.at[row_ids].add(gate_pad[pair_ids][:, None] * result.astype(jnp.float32)), None)
    summed, unused = lax.scan(step_fn, jnp.zeros((token_count + 1, D), jnp.float32), (pair_table, w_gate, w_up, w_down))
    mixed_sum = token_flat.astype(jnp.float32) + summed[:token_count]
    mixed_rows = mixed_sum.astype(jnp.bfloat16)
    return (mixed_sum.reshape(GROUPS, SAMPLES, SEQ, D), mixed_rows.reshape(GROUPS, SAMPLES, SEQ, D), gate_values, pair_table)

def reference(prompt_states, edit_offsets, targets, router, route_ids, chosen, lengths, w_gate, w_up, w_down):
    token_count = GROUPS * SAMPLES * SEQ
    tokens_now = prompt_states
    tables_all = []
    token_pads = []
    target_pads = []
    coef_pads = []
    advantage_list = []
    positions = jnp.arange(SEQ, dtype=jnp.int32)
    for turn_index in range(ROUNDS):
        mixed_sum, mixed_rows, gate_values, pair_table = forward_round(tokens_now, route_ids[turn_index], router, w_gate, w_up, w_down)
        scores = lax.optimization_barrier(jnp.sum(mixed_sum * targets[turn_index].astype(jnp.float32), axis=3)) / math.sqrt(D)
        valid_mask = (positions[None, None, :] < lengths[turn_index][..., None]).astype(jnp.float32)
        reward = lax.optimization_barrier(jnp.sum(valid_mask * scores, axis=2)) / lengths[turn_index].astype(jnp.float32)
        advantage = reward - lax.optimization_barrier(jnp.mean(reward, axis=1, keepdims=True))
        coef = (advantage[..., None, None] * valid_mask[..., None] * gate_values.astype(jnp.float32)).astype(jnp.bfloat16)
        tables_all.append(pair_table)
        token_pads.append(padded(tokens_now.reshape(token_count, D), (D,)))
        target_pads.append(padded(targets[turn_index].reshape(token_count, D), (D,)))
        coef_pads.append(padded(coef.reshape(token_count * TOP), ()))
        advantage_list.append(advantage)
        if turn_index + 1 < ROUNDS:
            best_rows = mixed_rows[jnp.arange(GROUPS, dtype=jnp.int32), chosen[turn_index]]
            tokens_now = (best_rows[:, None].astype(jnp.float32) + edit_offsets[turn_index].astype(jnp.float32)).astype(jnp.bfloat16)
    stacked_tables = jnp.stack(tables_all, axis=1)

    def grad_step(carry, inputs):
        table_rounds, gate_weight, up_weight, down_weight = inputs
        grad_gate = jnp.zeros((D, FF), jnp.float32)
        grad_up = jnp.zeros((D, FF), jnp.float32)
        grad_down = jnp.zeros((FF, D), jnp.float32)
        for turn_index in range(ROUNDS):
            pair_ids = table_rounds[turn_index]
            row_ids = pair_ids // TOP
            expert_rows = token_pads[turn_index][row_ids]
            pre_gate, pre_up, hidden, unused = expert_pass(expert_rows, gate_weight, up_weight, down_weight)
            cotangent = (coef_pads[turn_index][pair_ids].astype(jnp.float32)[:, None] * target_pads[turn_index][row_ids].astype(jnp.float32)).astype(jnp.bfloat16)
            grad_down = grad_down + jnp.dot(hidden.T, cotangent, preferred_element_type=jnp.float32)
            hidden_grad = jnp.dot(cotangent, down_weight.T, preferred_element_type=jnp.float32)
            sigmoid_gate = jax.nn.sigmoid(pre_gate)
            gate_grad = (hidden_grad * pre_up * sigmoid_gate * (1.0 + pre_gate * (1.0 - sigmoid_gate))).astype(jnp.bfloat16)
            up_grad = (hidden_grad * pre_gate * sigmoid_gate).astype(jnp.bfloat16)
            grad_gate = grad_gate + jnp.dot(expert_rows.T, gate_grad, preferred_element_type=jnp.float32)
            grad_up = grad_up + jnp.dot(expert_rows.T, up_grad, preferred_element_type=jnp.float32)
        return (carry, (grad_gate.astype(jnp.bfloat16), grad_up.astype(jnp.bfloat16), grad_down.astype(jnp.bfloat16)))
    unused, grads = lax.scan(grad_step, jnp.zeros((), jnp.float32), (stacked_tables, w_gate, w_up, w_down))
    return (grads[0], grads[1], grads[2], jnp.stack(advantage_list))
```

```python
import functools
import math

import jax
import jax.numpy as jnp
from jax import lax
from jax.experimental import pallas as pl
from jax.experimental.pallas import tpu as pltpu
from jax.sharding import PartitionSpec as P

F32 = jnp.float32
BF16 = jnp.bfloat16


def dot(a, b):
    return jnp.dot(a, b, preferred_element_type=F32)


def dot_tn(a, b):
    return lax.dot_general(a, b, (((0,), (0,)), ((), ())), preferred_element_type=F32)


def dot_nt(a, b):
    return lax.dot_general(a, b, (((1,), (1,)), ((), ())), preferred_element_type=F32)


MESH = pl.DeviceIdType.MESH
VMEM = pl.BlockSpec(memory_space=pltpu.VMEM)
ANY = pl.BlockSpec(memory_space=pl.ANY)


def greet(peers):
    barrier = pltpu.get_barrier_semaphore()
    for peer in peers:
        pl.semaphore_signal(barrier, inc=1, device_id=peer, device_id_type=MESH)
    pl.semaphore_wait(barrier, len(peers))


def remote(src, dst, send, recv, peer):
    return pltpu.make_async_remote_copy(
        src_ref=src, dst_ref=dst, send_sem=send, recv_sem=recv, device_id=peer, device_id_type=MESH
    )


def add_all(terms):
    total = terms[0]
    for term in terms[1:]:
        total = total + term
    return total


def round_kernel(
    ns, ng, seq, top, block, cap, rounds, extra, chunks, length_ref, chosen_ref, ids_ref, base_hbm, edit_hbm,
    target_hbm, router_hbm, gate_hbm, up_hbm, down_hbm, *refs
):
    count = 2 * rounds
    lands, mixed_ref, gate_pre, up_pre = refs[:count], refs[count], refs[count + 1], refs[count + 2]
    rest = list(refs[count + 3 :])
    alls, pairs, sends = rest[:count], rest[count : 2 * count], rest[2 * count : 2 * count + 2]
    (
        code, codes, place, router_ref, gate_w, up_w, down_w, hidden_ref, result_ref, rows_in, half, cols_in,
        final, load_sem, code_sem, line_sem, gs, gr, bs, br, fs, fr, rs, rr, ss, sr, sems_a, sems_b,
    ) = rest[2 * count + 2 :]
    width = base_hbm.shape[1]
    experts = ns * ng
    tokens = ng * seq
    rows = ns * block
    nl = ns // 4
    fan = 2 * nl
    me_s, me_g = lax.axis_index("samp"), lax.axis_index("exp")
    my_y, my_x, my_l = me_s // fan, lax.rem(me_s // nl, 2), lax.rem(me_s, nl)
    my_expert = me_s * ng + me_g

    def samp_at(y, x, l):
        return (y * 2 + x) * nl + l

    partners = [samp_at(1 - my_y, my_x, my_l), samp_at(my_y, 1 - my_x, my_l)]
    exp_peers = [(me_s, lax.rem(me_g + k, ng)) for k in range(1, ng)]
    samp_peers = [(lax.rem(me_s + k, ns), me_g) for k in range(1, ns)]
    mine = pl.ds(pl.multiple_of(me_g * seq, seq), seq)

    def rows_of(d):
        return pl.ds(pl.multiple_of(d * block, block), block)

    loads = [
        pltpu.make_async_copy(source, target, load_sem.at[n])
        for n, (source, target) in enumerate(
            [(base_hbm, alls[0].at[mine, :width])]
            + [(target_hbm.at[0], alls[rounds].at[mine, :])]
            + [(edit_hbm.at[r - 1], alls[r].at[mine, :width]) for r in range(1, rounds)]
            + [(target_hbm.at[r], alls[rounds + r].at[mine, :]) for r in range(1, rounds)]
            + [(base_hbm, result_ref.at[block:, :])]
            + [(router_hbm, router_ref), (gate_hbm, gate_w), (up_hbm, up_w), (down_hbm, down_w)]
        )
    ]
    for copy in loads:
        copy.start()

    lane_p = lax.broadcasted_iota(jnp.int32, (seq, experts), 1).astype(F32)
    block_p = jnp.floor((lane_p + 0.5) / ns)
    order_p = (lane_p - block_p * ns) * ng + block_p
    lane_m = lax.broadcasted_iota(jnp.int32, (seq, extra), 1)
    position = lax.broadcasted_iota(jnp.int32, (seq, extra), 0)
    hits = []
    for r in range(rounds):
        ids = ids_ref[r]
        ids_f = ids.astype(F32)
        hits.append(add_all([jnp.where(ids_f[:, k : k + 1] == order_p, 1.0, 0.0) for k in range(top)]))
        length = jnp.zeros((seq, extra), jnp.int32) + length_ref[r]
        info = jnp.where(lane_m == experts, position, 0)
        info = info + jnp.where((lane_m == experts + 1) & (position < length), 1, 0)
        info = info + jnp.where(lane_m == experts + 2, length, 0)
        info = info + jnp.where(lane_m == experts + 3, 1, 0)
        for k in range(top):
            info = info + jnp.where(ids[:, k : k + 1] == lane_m, 1, 0)
        alls[r][mine, width:] = info.astype(F32).astype(BF16)
    hit = jnp.concatenate(hits, axis=0).astype(BF16)
    long = rounds * seq
    row_t = lax.broadcasted_iota(jnp.int32, (long, long), 0)
    col_t = lax.broadcasted_iota(jnp.int32, (long, long), 1)
    same = row_t == col_t
    upto = jnp.zeros((long, long), F32)
    for r in range(rounds):
        lo, hi = r * seq, (r + 1) * seq
        inside = (row_t >= lo) & (row_t < hi) & (col_t >= lo) & (col_t < hi) & (row_t <= col_t)
        upto = upto + jnp.where(inside, 1.0, 0.0)
    rank = dot_tn(hit, upto.astype(BF16)) - 1.0
    own = dot_tn(hit, jnp.where(same, 1.0, 0.0).astype(BF16))
    offset = (jnp.zeros((experts, long), jnp.int32) + me_g * cap).astype(F32)
    line = jnp.where(own > 0.5, rank + offset, -1.0)
    for g in range(ng):
        code[g] = line[g * ns : (g + 1) * ns, :]
    codes[0, me_g] = code[me_g]
    greet(exp_peers + samp_peers)

    def gather_copies(c):
        i, lo, mid, hi, quota = chunks[c]
        part = alls[i].at[mine, lo:hi]
        copies = [remote(part, part, gs.at[c, k], gr.at[c, k], p) for k, p in enumerate(exp_peers)]
        ahead = []
        if quota:
            for h, (a, b) in enumerate([(mid - quota, mid), (mid, mid + quota)]):
                ahead.append(
                    remote(
                        alls[i].at[mine, a:b], pairs[i].at[mine, a:b], bs.at[c, h], br.at[c, h], (partners[h], me_g)
                    )
                )
        return copies, ahead

    def forward_copies(c):
        i, lo, mid, hi, quota = chunks[c]
        part = pairs[i].at[mine, mid - quota : mid + quota]
        return [remote(part, part, fs.at[c, k], fr.at[c, k], p) for k, p in enumerate(exp_peers)] if quota else []

    def relay_copies(c):
        i, lo, mid, hi, quota = chunks[c]
        return [
            remote(alls[i].at[:, a:b], pairs[i].at[:, a:b], rs.at[c, h], rr.at[c, h], (partners[h], me_g))
            for h, (a, b) in enumerate([(lo, mid - quota), (mid + quota, hi)])
        ]

    def start_gather(c):
        if c < len(chunks):
            if c == 0:
                loads[0].wait()
            elif chunks[c][0] != chunks[c - 1][0]:
                loads[order.index(chunks[c][0])].wait()
            copies, ahead = gather_copies(c)
            for copy in ahead + copies:
                copy.start()

    order = [0, rounds] + list(range(1, rounds)) + list(range(rounds + 1, count))

    def relay(c):
        copies, ahead = gather_copies(c)
        for copy in ahead:
            copy.wait()
        for copy in forward_copies(c):
            copy.start()
        for copy in copies:
            copy.wait()
        for copy in relay_copies(c):
            copy.start()
        start_gather(c + 1)

    def dest_of(h, k):
        l = lax.rem(my_l + lax.rem(k, nl), nl)
        if h == 0:
            return samp_at(my_y, lax.rem(my_x + k // nl, 2), l)
        return samp_at(lax.rem(my_y + k // nl, 2), my_x, l)

    def slot_copy(c, h, k, b):
        i, lo, mid, hi, quota = chunks[c]
        a, e = ((lo, mid), (mid, hi))[h]
        source = sends[i // rounds].at[rows_of(k * 2 + b), a:e]
        home = me_s if b == 0 else partners[h]
        return remote(
            source, lands[i].at[rows_of(home), a:e], ss.at[c, h, k, b], sr.at[c, h, k, b], (dest_of(h, k), me_g)
        )

    def scatter(c):
        i, lo, mid, hi, quota = chunks[c]
        for copy in relay_copies(c) + forward_copies(c):
            copy.wait()

        def placed(h, d, b):
            a, e = ((lo, mid), (mid, hi))[h]
            tokens_ref = alls[i] if b == 0 else pairs[i]
            return dot(place[i % rounds, 0 if b == 0 else 1 + h, rows_of(d), :], tokens_ref[:, a:e]).astype(BF16)

        def step(n, carry):
            k = fan - n
            for h in range(2):
                a, e = ((lo, mid), (mid, hi))[h]
                for b in range(2):
                    sends[i // rounds][rows_of(k * 2 + b), a:e] = placed(h, dest_of(h, k), b)
                    slot_copy(c, h, k, b).start()
            return carry

        lax.fori_loop(1, fan, step, 0)
        for h in range(2):
            a, e = ((lo, mid), (mid, hi))[h]
            for b in range(2):
                home = me_s if b == 0 else partners[h]
                lands[i][rows_of(home), a:e] = placed(h, me_s, b)

    def landed(c):
        def step(k, carry):
            for h in range(2):
                for b in range(2):
                    slot_copy(c, h, k, b).wait()
            return carry

        lax.fori_loop(1, fan, step, 0)

    start_gather(0)
    code_copies = [
        remote(code.at[peer[1]], codes.at[0, me_g], code_sem.at[0, k], code_sem.at[1, k], peer)
        for k, peer in enumerate(exp_peers)
    ]
    for copy in code_copies:
        copy.start()
    for copy in code_copies:
        copy.wait()
    line_copies = [
        remote(codes.at[0], codes.at[1 + h], line_sem.at[0, h], line_sem.at[1, h], (partners[h], me_g))
        for h in range(2)
    ]
    for copy in line_copies:
        copy.start()
    relay(0)
    for copy in line_copies:
        copy.wait()
    slots = lax.broadcasted_iota(jnp.int32, (block, tokens), 0).astype(F32)
    for r in range(rounds):
        for who in range(3):
            line = jnp.concatenate([codes[who, g][:, r * seq : (r + 1) * seq] for g in range(ng)], axis=1)
            for d in range(ns):
                hit = jnp.where(line[d : d + 1, :] == slots, 1.0, 0.0)
                place[r, who, d * block : (d + 1) * block, :] = hit.astype(BF16)
    relay(1)
    scatter(0)
    relay(2)
    scatter(1)
    for copy in loads[count:]:
        copy.wait()
    landed(0)
    landed(1)

    land = lands[0]
    tile = 256

    def project(n, carry):
        cols = pl.ds(pl.multiple_of(n * tile, tile), tile)
        pre_gate = dot(land[:, :width], gate_w[:, cols])
        pre_up = dot(land[:, :width], up_w[:, cols])
        gate_pre[:, cols] = pre_gate
        up_pre[:, cols] = pre_up
        hidden_ref[:, cols] = (pre_gate * jax.nn.sigmoid(pre_gate) * pre_up).astype(BF16)
        return carry

    lax.fori_loop(0, gate_w.shape[1] // tile, project, 0)
    scatter(2)

    def meta_rows(ref):
        lane = lax.broadcasted_iota(jnp.int32, (rows, experts), 1)
        mask = ref[:, width : width + experts].astype(F32) > 0.5
        first = (experts // 128) * 128
        last = ref[:, width + first : width + first + 128].astype(F32)
        lane_i = lax.broadcasted_iota(jnp.int32, (rows, 128), 1)
        info = [
            jnp.sum(jnp.where(lane_i == experts - first + n, last, 0.0), axis=1, keepdims=True) for n in range(4)
        ]
        return lane, mask, info

    lane, mask, info = meta_rows(land)
    sig = jnp.where(mask, jax.nn.sigmoid(dot(land[:, :width], router_ref[...])), 0.0)
    used = info[3] > 0.5
    total = jnp.where(used, jnp.sum(sig, axis=1, keepdims=True), 1.0)
    share = jnp.sum(jnp.where(lane == my_expert, sig, 0.0), axis=1, keepdims=True)
    gate = (share / total).astype(BF16).astype(F32)
    slot = lax.broadcasted_iota(jnp.int32, (block, 1), 0)
    slot_group = add_all([jnp.where(slot >= g * cap, 1, 0) for g in range(1, ng)])
    choice = add_all([jnp.where(slot_group == g, chosen_ref[0, g], 0) for g in range(ng)])
    hidden_sel = jnp.zeros((block, gate_w.shape[1]), F32)
    gate_sel = jnp.zeros((block, 1), F32)
    spot_sel = jnp.zeros((block, 1), F32)
    spot = jnp.where(used, info[0], -float(tokens))
    for d in range(ns):
        keep = choice == d
        at = slice(d * block, (d + 1) * block)
        hidden_sel = hidden_sel + jnp.where(keep, hidden_ref[at, :].astype(F32), 0.0)
        gate_sel = gate_sel + jnp.where(keep, gate[at], 0.0)
        spot_sel = spot_sel + jnp.where(keep, spot[at], 0.0)
    spot_sel = spot_sel + (slot_group * seq).astype(F32)
    result_ref[:block, :] = dot(hidden_sel.astype(BF16), down_w[...]).astype(BF16)
    token = lax.broadcasted_iota(jnp.int32, (block, tokens), 1).astype(F32)
    spread = jnp.where(spot_sel == token, gate_sel, 0.0)
    lead = lax.broadcasted_iota(jnp.int32, (seq, tokens), 0) + me_g * seq
    at_token = lax.broadcasted_iota(jnp.int32, (seq, tokens), 1)
    best = jnp.zeros((seq, tokens), jnp.int32) + chosen_ref[0, me_g]
    start = jnp.where((lead == at_token) & (best == me_s), 1.0, 0.0)
    combine = jnp.concatenate([spread, start], axis=0).astype(BF16)
    part_ref = sends[0].at[:tokens, :width]
    part_ref[...] = dot_tn(combine, result_ref[...]).astype(BF16)

    high = rows_in.shape[1]
    wide = width // ng

    def high_of(d):
        return pl.ds(pl.multiple_of(d * high, high), high)

    def cols_of(g):
        return pl.ds(pl.multiple_of(g * wide, wide), wide)

    copies = [
        remote(part_ref.at[high_of(peer[0]), :], rows_in.at[k], sems_a.at[0, k], sems_a.at[1, k], peer)
        for k, peer in enumerate(samp_peers)
    ]
    for copy in copies:
        copy.start()
    half[...] = part_ref[high_of(me_s), :].astype(F32)
    relay(3)
    for k, copy in enumerate(copies):
        copy.wait()
        half[...] += rows_in[k].astype(F32)
    copies = [
        remote(half.at[:, cols_of(peer[1])], cols_in.at[k], sems_b.at[0, k], sems_b.at[1, k], peer)
        for k, peer in enumerate(exp_peers)
    ]
    for copy in copies:
        copy.start()
    scatter(3)
    total = half[:, cols_of(me_g)]
    for k, copy in enumerate(copies):
        copy.wait()
        total = total + cols_in[k]
    final[...] = total.astype(BF16)
    mixed_ref[high_of(me_s), cols_of(me_g)] = final[...]
    copies = [
        remote(final, mixed_ref.at[high_of(me_s), cols_of(me_g)], sems_b.at[2, k], sems_b.at[3, k], peer)
        for k, peer in enumerate(exp_peers)
    ]
    for copy in copies:
        copy.start()
    relay(4)
    for copy in copies:
        copy.wait()
    copies = [
        remote(
            mixed_ref.at[high_of(me_s), :], mixed_ref.at[high_of(me_s), :], sems_a.at[2, k], sems_a.at[3, k], peer
        )
        for k, peer in enumerate(samp_peers)
    ]
    for copy in copies:
        copy.start()
    landed(2)
    scatter(4)
    for copy in copies:
        copy.wait()
    landed(3)
    landed(4)


def round_call(
    lengths, chosen, ids, base, edits, targets, router, gate_weight, up_weight, down_weight, ns, ng, block, cap
):
    rounds, seq, top = ids.shape
    width, experts = router.shape
    hidden = gate_weight.shape[1]
    extra = -(-(experts + 4) // 128) * 128
    rows, tokens = ns * block, ng * seq
    full = width + extra
    half, quarter = width // 2, width // 4
    chunks = [
        (0, 0, quarter, half, quarter // 2),
        (0, half, half + quarter, full, quarter // 2),
        (rounds, 0, half, width, 3 * half // 8),
        (1, 0, half, full, 3 * half // 8),
        (rounds + 1, 0, half, width, 3 * half // 8),
    ]
    steps = len(chunks)
    widths = [full] * rounds + [width] * rounds
    smem = pl.BlockSpec(memory_space=pltpu.SMEM)
    high = tokens // ns
    dma = pltpu.SemaphoreType.DMA
    return pl.pallas_call(
        functools.partial(round_kernel, ns, ng, seq, top, block, cap, rounds, extra, chunks),
        out_shape=[jax.ShapeDtypeStruct((rows, w), BF16) for w in widths]
        + [jax.ShapeDtypeStruct((tokens, width), BF16)]
        + [jax.ShapeDtypeStruct((rows, hidden), F32)] * 2,
        in_specs=[smem, smem, VMEM] + [ANY] * 7,
        out_specs=[VMEM] * (2 * rounds + 3),
        scratch_shapes=[pltpu.VMEM((tokens, w), BF16) for w in widths] * 2
        + [pltpu.VMEM((rows, full), BF16), pltpu.VMEM((rows, width), BF16)]
        + [
            pltpu.VMEM((ng, ns, rounds * seq), F32),
            pltpu.VMEM((3, ng, ns, rounds * seq), F32),
            pltpu.VMEM((rounds, 3, rows, tokens), BF16),
            pltpu.VMEM(router.shape, BF16),
            pltpu.VMEM(gate_weight.shape, BF16),
            pltpu.VMEM(up_weight.shape, BF16),
            pltpu.VMEM(down_weight.shape, BF16),
            pltpu.VMEM((rows, hidden), BF16),
            pltpu.VMEM((block + seq, width), BF16),
            pltpu.VMEM((ns - 1, high, width), BF16),
            pltpu.VMEM((high, width), F32),
            pltpu.VMEM((ng - 1, high, width // ng), F32),
            pltpu.VMEM((high, width // ng), BF16),
            dma((2 * rounds + 5,)),
            dma((2, ng - 1)),
            dma((2, 2)),
            dma((steps, ng - 1)),
            dma((steps, ng - 1)),
            dma((steps, 2)),
            dma((steps, 2)),
            dma((steps, ng - 1)),
            dma((steps, ng - 1)),
            dma((steps, 2)),
            dma((steps, 2)),
            dma((steps, 2, ns // 2, 2)),
            dma((steps, 2, ns // 2, 2)),
            dma((4, ns - 1)),
            dma((4, ng - 1)),
        ],
        compiler_params=pltpu.CompilerParams(
            collective_id=0, has_side_effects=True, vmem_limit_bytes=62 * 2**20
        ),
    )(lengths, chosen, ids, base, edits, targets, router, gate_weight, up_weight, down_weight)


def total_kernel(ns, ng, mine_ref, out_ref, slots, sends, recvs):
    me = lax.axis_index("samp") * ng + lax.axis_index("exp")
    devices = ns * ng
    barrier = pltpu.get_barrier_semaphore()

    def peer_of(k):
        index = lax.rem(me + k, devices)
        return (index // ng, lax.rem(index, ng))

    def hello(k, carry):
        pl.semaphore_signal(barrier, inc=1, device_id=peer_of(k), device_id_type=MESH)
        return carry

    lax.fori_loop(1, devices, hello, 0)
    pl.semaphore_wait(barrier, devices - 1)

    def copy_of(k):
        return remote(mine_ref, slots.at[me], sends.at[k], recvs.at[k], peer_of(k))

    def send(k, carry):
        copy_of(k).start()
        return carry

    lax.fori_loop(1, devices, send, 0)
    slots[me] = mine_ref[...]

    def take(k, carry):
        copy_of(k).wait()
        return carry

    lax.fori_loop(1, devices, take, 0)
    out_ref[...] = jnp.sum(slots[...], axis=0)


def total_of(values, ns, ng):
    devices = ns * ng
    return pl.pallas_call(
        functools.partial(total_kernel, ns, ng),
        out_shape=jax.ShapeDtypeStruct(values.shape, F32),
        in_specs=[VMEM],
        out_specs=VMEM,
        scratch_shapes=[
            pltpu.VMEM((devices,) + values.shape, F32),
            pltpu.SemaphoreType.DMA((devices,)),
            pltpu.SemaphoreType.DMA((devices,)),
        ],
        compiler_params=pltpu.CompilerParams(collective_id=2, has_side_effects=True),
    )(values)


def per_device(
    prompt_states, edit_offsets, targets, router, route_ids, chosen, lengths, w_gate, w_up, w_down
):
    seq = prompt_states.shape[2]
    width = prompt_states.shape[3]
    rounds = route_ids.shape[0]
    top = route_ids.shape[4]
    experts = router.shape[1]
    cap = seq * top * 5 // (4 * experts)
    samplers = lax.axis_size("samp")
    groups = lax.axis_size("exp")
    my_samp = lax.axis_index("samp")
    my_group = lax.axis_index("exp")
    my_expert = my_samp * groups + my_group
    block = -(-groups * cap // 16) * 16
    rows = samplers * block
    tokens = groups * seq
    gate_weight, up_weight, down_weight = w_gate[0], w_up[0], w_down[0]
    expert_iota = jnp.arange(experts, dtype=jnp.int32)
    positions = jnp.arange(seq, dtype=jnp.int32)

    row_iota = jnp.arange(rows, dtype=jnp.int32)
    row_group = jnp.minimum((row_iota % block) // cap, groups - 1)
    row_repair = row_iota // block * groups + row_group
    repair_onehot = row_repair[:, None] == jnp.arange(samplers * groups, dtype=jnp.int32)[None, :]
    token_iota = jnp.arange(tokens, dtype=jnp.int32)

    def columns_of(meta):
        info = meta[:, experts : experts + 4].astype(F32)
        used = info[:, 3] > 0.5
        return meta[:, :experts] > 0.5, info[:, 0].astype(jnp.int32), info[:, 1], info[:, 2], used

    def gates_of(received, mask, used):
        logits = dot(received, router)
        sig = jnp.where(mask, jax.nn.sigmoid(logits), 0.0)
        total = jnp.where(used, jnp.sum(sig, axis=1), 1.0)
        own = jnp.sum(jnp.where(expert_iota[None, :] == my_expert, sig, 0.0), axis=1)
        return (own / total).astype(BF16)

    def own_part(x, target, r):
        length = lengths[r, 0, 0]
        valid = (positions < length).astype(F32)
        score = jnp.sum(x.astype(F32) * target.astype(F32), axis=1) / math.sqrt(width)
        return jnp.sum(valid * score) / length.astype(F32)

    def reward_part(hidden, back, gate, valid, length, used, own):
        score = jnp.sum(hidden.astype(F32) * back, axis=1) / math.sqrt(width)
        score = gate.astype(F32) * valid * score / jnp.where(used, length, 1.0)
        part = jnp.sum(jnp.where(repair_onehot, score[:, None], 0.0), axis=0)
        repairs = jnp.arange(samplers * groups, dtype=jnp.int32)
        return part + jnp.where(repairs == my_expert, own, 0.0)

    bases = [prompt_states[0, 0]] + [edit_offsets[r, 0, 0] for r in range(rounds - 1)]
    *landed, mixed, first_gate, first_up = round_call(
        lengths.reshape(rounds),
        chosen,
        route_ids[:, 0, 0],
        bases[0],
        edit_offsets[:, 0, 0],
        targets[:, 0, 0],
        router,
        gate_weight,
        up_weight,
        down_weight,
        samplers,
        groups,
        block,
        cap,
    )
    parts = []
    saved = []
    for r in range(rounds):
        arrived, target_rows = landed[r], landed[rounds + r]
        mask, row_pos, valid, length, used = columns_of(arrived[:, width:])
        received = arrived[:, :width]
        token_code = jnp.where(used, row_group * seq + row_pos, -1)
        own_x = bases[r]
        if r > 0:
            lift = (token_code[:, None] == token_iota[None, :]).astype(BF16)
            received = (dot(lift, mixed) + received.astype(F32)).astype(BF16)
            best = lax.dynamic_slice_in_dim(mixed, my_group * seq, seq, axis=0)
            own_x = (best.astype(F32) + own_x.astype(F32)).astype(BF16)
        gate = gates_of(received, mask, used)
        if r == 0:
            pre_gate, pre_up = first_gate, first_up
        else:
            pre_gate = dot(received, gate_weight)
            pre_up = dot(received, up_weight)
        hidden = (jax.nn.silu(pre_gate) * pre_up).astype(BF16)
        back = dot_nt(target_rows, down_weight)
        parts.append(
            reward_part(
                hidden, back, gate, valid, length, used, own_part(own_x, targets[r, 0, 0], r)
            )
        )
        saved.append((received, target_rows, gate, valid, pre_gate, pre_up, hidden, back))
    filled = jnp.zeros((8, -(-samplers * groups // 128) * 128), F32)
    filled = filled.at[:rounds, : samplers * groups].set(jnp.stack(parts))
    rewards = total_of(filled, samplers, groups)[:rounds, : samplers * groups]
    rewards = rewards.reshape(rounds, samplers, groups)
    advantage = rewards - jnp.mean(rewards, axis=1, keepdims=True)
    flat = advantage.reshape(rounds, samplers * groups)
    grad_gate = grad_up = grad_down = 0.0
    for r, (received, target_rows, gate, valid, pre_gate, pre_up, hidden, back) in enumerate(saved):
        row_adv = jnp.sum(jnp.where(repair_onehot, flat[r][None, :], 0.0), axis=1)
        coef = (row_adv * valid * gate.astype(F32)).astype(BF16).astype(F32)[:, None]
        hidden_grad = coef * back
        sg = jax.nn.sigmoid(pre_gate)
        gate_grad = (hidden_grad * pre_up * sg * (1.0 + pre_gate * (1.0 - sg))).astype(BF16)
        up_grad = (hidden_grad * pre_gate * sg).astype(BF16)
        weighted = (hidden.astype(F32) * coef).astype(BF16)
        grad_down = grad_down + dot_tn(weighted, target_rows)
        grad_gate = grad_gate + dot_tn(received, gate_grad)
        grad_up = grad_up + dot_tn(received, up_grad)
    repairs = jnp.arange(samplers * groups, dtype=jnp.int32)
    my_adv = jnp.sum(jnp.where(repairs[None, :] == my_expert, flat, 0.0), axis=1)
    return (
        grad_gate.astype(BF16)[None],
        grad_up.astype(BF16)[None],
        grad_down.astype(BF16)[None],
        my_adv.reshape(rounds, 1, 1),
    )


def solution(mesh):
    placed = (
        P("exp", "samp", None, None),
        P(None, "exp", "samp", None, None),
        P(None, "exp", "samp", None, None),
        P(),
        P(None, "exp", "samp", None, None),
        P(),
        P(None, "exp", "samp"),
        P(("samp", "exp"), None, None),
        P(("samp", "exp"), None, None),
        P(("samp", "exp"), None, None),
    )
    return jax.shard_map(
        per_device,
        mesh=mesh,
        in_specs=placed,
        out_specs=(
            P(("samp", "exp"), None, None),
            P(("samp", "exp"), None, None),
            P(("samp", "exp"), None, None),
            P(None, "exp", "samp"),
        ),
        check_vma=False,
    )
```

```python
import functools
import math

import jax
import jax.numpy as jnp
from jax import lax
from jax.experimental import pallas as pl
from jax.experimental.pallas import tpu as pltpu
from jax.sharding import PartitionSpec as P

F32 = jnp.float32
BF16 = jnp.bfloat16


def dot(a, b):
    return jnp.dot(a, b, preferred_element_type=F32)


def dot_tn(a, b):
    return lax.dot_general(a, b, (((0,), (0,)), ((), ())), preferred_element_type=F32)


def dot_nt(a, b):
    return lax.dot_general(a, b, (((1,), (1,)), ((), ())), preferred_element_type=F32)


MESH = pl.DeviceIdType.MESH
VMEM = pl.BlockSpec(memory_space=pltpu.VMEM)
ANY = pl.BlockSpec(memory_space=pl.ANY)


def greet(peers):
    barrier = pltpu.get_barrier_semaphore()
    for peer in peers:
        pl.semaphore_signal(barrier, inc=1, device_id=peer, device_id_type=MESH)
    pl.semaphore_wait(barrier, len(peers))


def remote(src, dst, send, recv, peer):
    return pltpu.make_async_remote_copy(
        src_ref=src, dst_ref=dst, send_sem=send, recv_sem=recv, device_id=peer, device_id_type=MESH
    )


def add_all(terms):
    total = terms[0]
    for term in terms[1:]:
        total = total + term
    return total


def step_kernel(ns, ng, seq, top, block, cap, rounds, extra, chunks, shared, *refs):
    count = 2 * rounds
    length_ref, chosen_ref, ids_ref = refs[:3]
    base_hbm, edit_hbm, target_hbm, router_hbm, gate_hbm, up_hbm, down_hbm = refs[3:10]
    outs, adv_ref = refs[10:15], refs[15]
    rest = list(refs[16:])

    def take(n):
        taken = rest[:n]
        del rest[:n]
        return taken

    lands, alls, pairs, sends = take(count), take(count), take(count), take(1 if shared else 2)
    (
        gate_act, up_act, hid_act, code, codes, lines, place, router_ref, gate_w, up_w, down_w, result_ref, mixed,
        core_in, sub, rows_in, half, cols_in, final, vote, vote_z, vote_s, load_sem, store_sem, code_sem, line_sem,
        gs, gr, rs, rr, ss, sr, core_sem, plane_sem, z_sem, vote_zs, vote_ss,
    ) = rest
    width = base_hbm.shape[1]
    hidden = gate_w.shape[1]
    experts = ns * ng
    tokens = ng * seq
    rows = ns * block
    nl = ns // 4
    fan = 2 * nl
    tile = 256
    lanes = vote.shape[-1]
    me_s, me_g = lax.axis_index("samp"), lax.axis_index("exp")
    my_y, my_x, my_l = me_s // fan, lax.rem(me_s // nl, 2), lax.rem(me_s, nl)
    my_expert = me_s * ng + me_g

    def samp_at(y, x, l):
        return (y * 2 + x) * nl + l

    partners = [samp_at(1 - my_y, my_x, my_l), samp_at(my_y, 1 - my_x, my_l)]
    exp_peers = [(me_s, lax.rem(me_g + k, ng)) for k in range(1, ng)]
    samp_peers = [(lax.rem(me_s + k, ns), me_g) for k in range(1, ns)]
    mine = pl.ds(pl.multiple_of(me_g * seq, seq), seq)

    def rows_of(d):
        return pl.ds(pl.multiple_of(d * block, block), block)

    loads = [
        pltpu.make_async_copy(source, target, load_sem.at[n])
        for n, (source, target) in enumerate(
            [(base_hbm, alls[0].at[mine, :width])]
            + [(target_hbm.at[0], alls[rounds].at[mine, :])]
            + [(edit_hbm.at[r - 1], alls[r].at[mine, :width]) for r in range(1, rounds)]
            + [(target_hbm.at[r], alls[rounds + r].at[mine, :]) for r in range(1, rounds)]
            + [(base_hbm, result_ref.at[block:, :])]
            + [(router_hbm, router_ref), (gate_hbm, gate_w), (up_hbm, up_w), (down_hbm, down_w)]
        )
    ]
    order = [0, rounds] + list(range(1, rounds)) + list(range(rounds + 1, count))
    for copy in loads:
        copy.start()

    lane_p = lax.broadcasted_iota(jnp.int32, (seq, experts), 1).astype(F32)
    block_p = jnp.floor((lane_p + 0.5) / ns)
    order_p = (lane_p - block_p * ns) * ng + block_p
    lane_m = lax.broadcasted_iota(jnp.int32, (seq, extra), 1)
    position = lax.broadcasted_iota(jnp.int32, (seq, extra), 0)
    hits = []
    for r in range(rounds):
        ids = ids_ref[r]
        ids_f = ids.astype(F32)
        hits.append(add_all([jnp.where(ids_f[:, k : k + 1] == order_p, 1.0, 0.0) for k in range(top)]))
        length = jnp.zeros((seq, extra), jnp.int32) + length_ref[r]
        info = jnp.where(lane_m == experts, position, 0)
        info = info + jnp.where((lane_m == experts + 1) & (position < length), 1, 0)
        info = info + jnp.where(lane_m == experts + 2, length, 0)
        info = info + jnp.where(lane_m == experts + 3, 1, 0)
        for k in range(top):
            info = info + jnp.where(ids[:, k : k + 1] == lane_m, 1, 0)
        alls[r][mine, width:] = info.astype(F32).astype(BF16)
    hit = jnp.concatenate(hits, axis=0).astype(BF16)
    long = rounds * seq
    row_t = lax.broadcasted_iota(jnp.int32, (long, long), 0)
    col_t = lax.broadcasted_iota(jnp.int32, (long, long), 1)
    same = row_t == col_t
    upto = jnp.zeros((long, long), F32)
    for r in range(rounds):
        lo, hi = r * seq, (r + 1) * seq
        inside = (row_t >= lo) & (row_t < hi) & (col_t >= lo) & (col_t < hi) & (row_t <= col_t)
        upto = upto + jnp.where(inside, 1.0, 0.0)
    rank = dot_tn(hit, upto.astype(BF16)) - 1.0
    own = dot_tn(hit, jnp.where(same, 1.0, 0.0).astype(BF16))
    offset = (jnp.zeros((experts, long), jnp.int32) + me_g * cap).astype(F32)
    line = jnp.where(own > 0.5, rank + offset, -1.0)
    for g in range(ng):
        code[g] = line[g * ns : (g + 1) * ns, :]
    codes[0, me_g] = code[me_g]
    greet(exp_peers + samp_peers)


    def gather_copies(c):
        i, lo, mid, hi = chunks[c]
        part = alls[i].at[mine, lo:hi]
        return [remote(part, part, gs.at[c, k], gr.at[c, k], p) for k, p in enumerate(exp_peers)]

    def relay_copies(c):
        i, lo, mid, hi = chunks[c]
        return [
            remote(alls[i].at[:, a:b], pairs[i].at[:, a:b], rs.at[c, h], rr.at[c, h], (partners[h], me_g))
            for h, (a, b) in enumerate([(lo, mid), (mid, hi)])
        ]

    def start(copies):
        for copy in copies:
            copy.start()
        return copies

    def finish(copies):
        for copy in copies:
            copy.wait()

    ready = set()

    def gather(c):
        if c < len(chunks):
            i = chunks[c][0]
            if i not in ready:
                ready.add(i)
                loads[order.index(i)].wait()
            start(gather_copies(c))

    def relay(c):
        finish(gather_copies(c))
        start(relay_copies(c))
        gather(c + 2)

    def dest_of(h, k):
        l = lax.rem(my_l + lax.rem(k, nl), nl)
        if h == 0:
            return samp_at(my_y, lax.rem(my_x + k // nl, 2), l)
        return samp_at(lax.rem(my_y + k // nl, 2), my_x, l)

    def cols_at(c, h):
        i, lo, mid, hi = chunks[c]
        return (lo, mid) if h == 0 else (mid, hi)

    def buffer_of(c):
        return sends[0 if shared else chunks[c][0] // rounds]

    def slot_copy(c, h, k, b):
        i = chunks[c][0]
        a, e = cols_at(c, h)
        home = me_s if b == 0 else partners[h]
        return remote(
            buffer_of(c).at[rows_of(b * fan + k), a:e],
            lands[i].at[rows_of(home), a:e],
            ss.at[c, h, k, b],
            sr.at[c, h, k, b],
            (dest_of(h, k), me_g),
        )

    done = set()

    def landed(c):
        if c in done:
            return
        done.add(c)

        def step(k, carry):
            for h in range(2):
                for b in range(2):
                    slot_copy(c, h, k, b).wait()
            return carry

        lax.fori_loop(1, fan, step, 0)

    def scatter(c):
        i = chunks[c][0]
        finish(relay_copies(c))
        for p in range(c):
            if (shared or chunks[p][0] // rounds == i // rounds) and chunks[p][1] == chunks[c][1]:
                landed(p)
        for h in range(2):
            a, e = cols_at(c, h)
            for b in range(2):
                tokens_ref = alls[i] if b == 0 else pairs[i]
                placed = dot(place[i % rounds, h, b], tokens_ref[:, a:e]).astype(BF16)
                buffer_of(c)[(b * fan + 1) * block : (b + 1) * fan * block, a:e] = placed[block:]
                home = me_s if b == 0 else partners[h]
                lands[i][rows_of(home), a:e] = placed[:block]

                def step(n, carry, h=h, b=b):
                    slot_copy(c, h, fan - n, b).start()
                    return carry

                lax.fori_loop(1, fan, step, 0)

    code_copies = start(
        [
            remote(code.at[peer[1]], codes.at[0, me_g], code_sem.at[0, k], code_sem.at[1, k], peer)
            for k, peer in enumerate(exp_peers)
        ]
    )
    gather(0)
    gather(1)
    finish(code_copies)
    line_copies = start(
        [
            remote(codes.at[0], codes.at[1 + h], line_sem.at[0, h], line_sem.at[1, h], (partners[h], me_g))
            for h in range(2)
        ]
    )
    relay(0)
    finish(line_copies)
    slots = lax.broadcasted_iota(jnp.int32, (block, tokens), 0).astype(F32)
    for r in range(rounds):
        for who in range(3):
            lines[r, who] = jnp.concatenate(
                [codes[who, g][:, r * seq : (r + 1) * seq] for g in range(ng)], axis=1
            )
        for h in range(2):
            for b in range(2):
                for k in range(fan):
                    line = lines[r, 0 if b == 0 else 1 + h, pl.ds(dest_of(h, k), 1), :]
                    hit = jnp.where(line == slots, 1.0, 0.0)
                    place[r, h, b, k * block : (k + 1) * block, :] = hit.astype(BF16)

    row_i = lax.broadcasted_iota(jnp.int32, (rows, 1), 0)
    row_samp = add_all([jnp.where(row_i >= d * block, 1, 0) for d in range(1, ns)])
    row_slot = row_i - row_samp * block
    row_group = add_all([jnp.where(row_slot >= g * cap, 1, 0) for g in range(1, ng)])
    lane_v = lax.broadcasted_iota(jnp.int32, (rows, lanes), 1)
    repair_hot = row_samp * ng + row_group == lane_v
    scale = 1.0 / math.sqrt(width)

    def stores(r, n):
        source = (lands[r].at[:, :width], lands[rounds + r], gate_act.at[r], up_act.at[r], hid_act.at[r])[n]
        target = outs[n].at[r * rows : (r + 1) * rows, :]
        return pltpu.make_async_copy(source, target, store_sem.at[r, n])

    def project(r):
        def step(n, carry):
            cols = pl.ds(pl.multiple_of(n * tile, tile), tile)
            pre_gate = dot(lands[r][:, :width], gate_w[:, cols])
            pre_up = dot(lands[r][:, :width], up_w[:, cols])
            sg = jax.nn.sigmoid(pre_gate)
            silu = pre_gate * sg
            hid_act[r, :, cols] = (silu * pre_up).astype(BF16)
            gate_act[r, :, cols] = (pre_up * sg * (1.0 + pre_gate * (1.0 - sg))).astype(BF16)
            up_act[r, :, cols] = silu.astype(BF16)
            return carry

        lax.fori_loop(0, hidden // tile, step, 0)

    def row_info(r):
        first = (experts // 128) * 128
        last = lands[r][:, width + first : width + first + 128].astype(F32)
        lane_i = lax.broadcasted_iota(jnp.int32, (rows, 128), 1)
        return [
            jnp.sum(jnp.where(lane_i == experts - first + n, last, 0.0), axis=1, keepdims=True) for n in range(4)
        ]

    def gates(r, used):
        lane = lax.broadcasted_iota(jnp.int32, (rows, experts), 1)
        mask = lands[r][:, width : width + experts].astype(F32) > 0.5
        sig = jnp.where(mask, jax.nn.sigmoid(dot(lands[r][:, :width], router_ref[...])), 0.0)
        total = jnp.where(used, jnp.sum(sig, axis=1, keepdims=True), 1.0)
        share = jnp.sum(jnp.where(lane == my_expert, sig, 0.0), axis=1, keepdims=True)
        return (share / total).astype(BF16).astype(F32)

    def backward(r):
        def step(n, score):
            cols = pl.ds(pl.multiple_of(n * tile, tile), tile)
            back = dot_nt(lands[rounds + r][...], down_w[cols, :])
            gate_act[r, :, cols] = (gate_act[r, :, cols].astype(F32) * back).astype(BF16)
            up_act[r, :, cols] = (up_act[r, :, cols].astype(F32) * back).astype(BF16)
            return score + jnp.sum(hid_act[r, :, cols].astype(F32) * back, axis=1, keepdims=True)

        return lax.fori_loop(0, hidden // tile, step, jnp.zeros((rows, 1), F32))

    def own_reward(r):
        x = alls[r][mine, :width].astype(F32)
        if r > 0:
            x = (x + mixed[mine, :].astype(F32)).astype(BF16).astype(F32)
        score = jnp.sum(x * alls[rounds + r][mine, :].astype(F32), axis=1, keepdims=True) * scale
        place_t = lax.broadcasted_iota(jnp.int32, (seq, 1), 0)
        score = jnp.where(place_t < length_ref[r], score, 0.0)
        length = (jnp.zeros((1, 1), jnp.int32) + length_ref[r]).astype(F32)
        return jnp.sum(score, axis=0, keepdims=True) / length

    def vote_copies(r, phase):
        if phase == 0:
            return [
                remote(vote.at[r, 0], vote_z.at[r, k], vote_zs.at[r, 0, k], vote_zs.at[r, 1, k], peer)
                for k, peer in enumerate(exp_peers)
            ]
        return [
            remote(vote.at[r, 1], vote_s.at[r, k], vote_ss.at[r, 0, k], vote_ss.at[r, 1, k], peer)
            for k, peer in enumerate(samp_peers)
        ]

    def vote_open(r, score, gate, info, own):
        used = info[3] > 0.5
        row_score = gate * info[1] * (score * scale) / jnp.where(used, info[2], 1.0)
        lane = lax.broadcasted_iota(jnp.int32, (8, lanes), 1)
        parts = jnp.sum(jnp.where(repair_hot, row_score, 0.0), axis=0, keepdims=True)
        vote[r, 0] = jnp.where(lane == my_expert, own, 0.0) + parts
        start(vote_copies(r, 0))

    def vote_pass(r):
        total = vote[r, 0]
        for k, copy in enumerate(vote_copies(r, 0)):
            copy.wait()
            total = total + vote_z[r, k]
        vote[r, 1] = total
        start(vote_copies(r, 1))

    def vote_close(r):
        total = vote[r, 1]
        for k, copy in enumerate(vote_copies(r, 1)):
            copy.wait()
            total = total + vote_s[r, k]
        lane = lax.broadcasted_iota(jnp.int32, (8, lanes), 1).astype(F32)
        group = lane - jnp.floor((lane + 0.5) / ng) * ng
        mean = jnp.zeros((8, lanes), F32)
        for g in range(ng):
            member = (group == g) & (lane < experts)
            sums = jnp.sum(jnp.where(member, total, 0.0), axis=1, keepdims=True)
            mean = mean + jnp.where(member, sums / ns, 0.0)
        advantage = total - mean
        lane_i = lax.broadcasted_iota(jnp.int32, (8, lanes), 1)
        my_adv = jnp.sum(jnp.where(lane_i == my_expert, advantage, 0.0), axis=1, keepdims=True)
        adv_ref[r] = jnp.broadcast_to(my_adv, (8, 128))
        return advantage

    def weigh(r, advantage, gate, info):
        row_adv = jnp.sum(jnp.where(repair_hot, advantage[:1, :], 0.0), axis=1, keepdims=True)
        coef = (row_adv * info[1] * gate).astype(BF16).astype(F32)
        for act in (gate_act, up_act, hid_act):
            act[r] = (act[r].astype(F32) * coef).astype(BF16)

    high = rows_in.shape[1]
    wide = width // ng
    tall = 4 * high
    my_yx = my_y * 2 + my_x
    my_part = my_l * 4 + my_yx

    def high_of(d):
        return pl.ds(pl.multiple_of(d * high, high), high)

    def tall_of(l):
        return pl.ds(pl.multiple_of(l * tall, tall), tall)

    def cols_of(g):
        return pl.ds(pl.multiple_of(g * wide, wide), wide)

    core_peers = [lax.rem(my_l + n, nl) for n in range(1, nl)]
    plane_peers = [lax.rem(my_yx + n, 4) for n in range(1, 4)]

    part = alls[0].at[:, :width]

    def mix_copies(phase):
        if phase == 0:
            pieces = [
                (part.at[tall_of(l), :], core_in.at[n], core_sem, n, (my_yx * nl + l, me_g))
                for n, l in enumerate(core_peers)
            ]
        elif phase == 1:
            pieces = [
                (sub.at[high_of(p), :], rows_in.at[n], plane_sem, n, (p * nl + my_l, me_g))
                for n, p in enumerate(plane_peers)
            ]
        elif phase == 2:
            pieces = [
                (half.at[:, cols_of(peer[1])], cols_in.at[n], z_sem, n, peer) for n, peer in enumerate(exp_peers)
            ]
        elif phase == 3:
            there = mixed.at[high_of(my_part), cols_of(me_g)]
            pieces = [(final, there, z_sem, n, peer) for n, peer in enumerate(exp_peers)]
        elif phase == 4:
            there = mixed.at[high_of(my_part), :]
            pieces = [(there, there, plane_sem, n, (p * nl + my_l, me_g)) for n, p in enumerate(plane_peers)]
        else:
            there = mixed.at[tall_of(my_l), :]
            pieces = [(there, there, core_sem, n, (my_yx * nl + l, me_g)) for n, l in enumerate(core_peers)]
        late = 2 if phase > 2 else 0
        return [remote(a, b, sem.at[late, n], sem.at[late + 1, n], peer) for a, b, sem, n, peer in pieces]

    relay(1)
    scatter(0)
    relay(2)
    scatter(1)
    relay(3)
    scatter(2)
    finish(loads[count:])
    landed(0)
    landed(1)
    stores(0, 0).start()
    project(0)
    relay(4)
    scatter(3)

    info_0 = row_info(0)
    used_0 = info_0[3] > 0.5
    gate_0 = gates(0, used_0)
    slot = lax.broadcasted_iota(jnp.int32, (block, 1), 0)
    slot_group = add_all([jnp.where(slot >= g * cap, 1, 0) for g in range(1, ng)])
    choice = add_all([jnp.where(slot_group == g, chosen_ref[0, g], 0) for g in range(ng)])
    hidden_sel = jnp.zeros((block, hidden), F32)
    gate_sel = jnp.zeros((block, 1), F32)
    spot_sel = jnp.zeros((block, 1), F32)
    spot = jnp.where(used_0, info_0[0], -float(tokens))
    for d in range(ns):
        keep = choice == d
        at = slice(d * block, (d + 1) * block)
        hidden_sel = hidden_sel + jnp.where(keep, hid_act[0, at, :].astype(F32), 0.0)
        gate_sel = gate_sel + jnp.where(keep, gate_0[at], 0.0)
        spot_sel = spot_sel + jnp.where(keep, spot[at], 0.0)
    spot_sel = spot_sel + (slot_group * seq).astype(F32)
    result_ref[:block, :] = dot(hidden_sel.astype(BF16), down_w[...]).astype(BF16)
    token = lax.broadcasted_iota(jnp.int32, (block, tokens), 1).astype(F32)
    spread = jnp.where(spot_sel == token, gate_sel, 0.0)
    lead = lax.broadcasted_iota(jnp.int32, (seq, tokens), 0) + me_g * seq
    at_token = lax.broadcasted_iota(jnp.int32, (seq, tokens), 1)
    best = jnp.zeros((seq, tokens), jnp.int32) + chosen_ref[0, me_g]
    own_hot = jnp.where((lead == at_token) & (best == me_s), 1.0, 0.0)
    combine = jnp.concatenate([spread, own_hot], axis=0).astype(BF16)
    own_0 = own_reward(0)
    part[...] = dot_tn(combine, result_ref[...]).astype(BF16)
    start(mix_copies(0))
    relay(5)
    finish(mix_copies(0))
    total = part[tall_of(my_l), :].astype(F32)
    for n in range(nl - 1):
        total = total + core_in[n].astype(F32)
    sub[...] = total.astype(BF16)
    start(mix_copies(1))
    scatter(4)
    finish(mix_copies(1))
    total = sub[high_of(my_yx), :].astype(F32)
    for n in range(3):
        total = total + rows_in[n].astype(F32)
    half[...] = total
    start(mix_copies(2))
    relay(6)
    scatter(5)
    finish(mix_copies(2))
    total = half[:, cols_of(me_g)]
    for n in range(ng - 1):
        total = total + cols_in[n]
    final[...] = total.astype(BF16)
    mixed[high_of(my_part), cols_of(me_g)] = final[...]
    start(mix_copies(3))
    landed(2)
    landed(3)
    stores(0, 1).start()
    relay(7)
    scatter(6)
    finish(mix_copies(3))
    start(mix_copies(4))
    score_0 = backward(0)
    finish(mix_copies(4))
    start(mix_copies(5))
    vote_open(0, score_0, gate_0, info_0, own_0)
    scatter(7)
    finish(mix_copies(5))
    vote_pass(0)
    landed(4)
    landed(5)

    info_1 = row_info(1)
    used_1 = info_1[3] > 0.5
    spot_1 = jnp.where(used_1, info_1[0] + (row_group * seq).astype(F32), -1.0)
    token_r = lax.broadcasted_iota(jnp.int32, (rows, tokens), 1).astype(F32)
    lift = jnp.where(spot_1 == token_r, 1.0, 0.0).astype(BF16)
    for n in range(0, width, 2 * tile):
        cols = slice(n, n + 2 * tile)
        lifted = dot(lift, mixed[:, cols]) + lands[1][:, cols].astype(F32)
        lands[1][:, cols] = lifted.astype(BF16)
    stores(1, 0).start()
    project(1)
    gate_1 = gates(1, used_1)
    weigh(0, vote_close(0), gate_0, info_0)
    for n in range(2, 5):
        stores(0, n).start()
    landed(6)
    landed(7)
    stores(1, 1).start()
    vote_open(1, backward(1), gate_1, info_1, own_reward(1))
    vote_pass(1)
    weigh(1, vote_close(1), gate_1, info_1)
    for n in range(2, 5):
        stores(1, n).start()
    for r in range(rounds):
        for n in range(5):
            stores(r, n).wait()


def step_call(
    lengths, chosen, ids, base, edits, targets, router, gate_weight, up_weight, down_weight, ns, ng, block, cap
):
    rounds, seq, top = ids.shape
    width, experts = router.shape
    hidden = gate_weight.shape[1]
    extra = -(-(experts + 4) // 128) * 128
    lanes = -(-experts // 128) * 128
    rows, tokens = ns * block, ng * seq
    full = width + extra
    half, quarter = width // 2, width // 4
    chunks = []
    for r in range(rounds):
        for i in (r, rounds + r):
            end = full if i < rounds else width
            chunks += [(i, 0, quarter, half), (i, half, half + quarter, end)]
    steps = len(chunks)
    widths = [full] * rounds + [width] * rounds
    smem = pl.BlockSpec(memory_space=pltpu.SMEM)
    nl = ns // 4
    high = tokens // ns
    shared = rows * tokens > 640 * 256
    dma = pltpu.SemaphoreType.DMA
    vm = pltpu.VMEM
    return pl.pallas_call(
        functools.partial(step_kernel, ns, ng, seq, top, block, cap, rounds, extra, chunks, shared),
        out_shape=[jax.ShapeDtypeStruct((rounds * rows, width), BF16)] * 2
        + [jax.ShapeDtypeStruct((rounds * rows, hidden), BF16)] * 3
        + [jax.ShapeDtypeStruct((rounds, 8, 128), F32)],
        in_specs=[smem, smem, VMEM] + [ANY] * 7,
        out_specs=[ANY] * 5 + [VMEM],
        scratch_shapes=[vm((rows, w), BF16) for w in widths]
        + [vm((tokens, w), BF16) for w in widths] * 2
        + [vm((rows, full), BF16)]
        + ([] if shared else [vm((rows, width), BF16)])
        + [vm((rounds, rows, hidden), BF16)] * 3
        + [
            vm((ng, ns, rounds * seq), F32),
            vm((3, ng, ns, rounds * seq), F32),
            vm((rounds, 3, ns, tokens), F32),
            vm((rounds, 2, 2, 2 * nl * block, tokens), BF16),
            vm(router.shape, BF16),
            vm(gate_weight.shape, BF16),
            vm(up_weight.shape, BF16),
            vm(down_weight.shape, BF16),
            vm((block + seq, width), BF16),
            vm((tokens, width), BF16),
            vm((nl - 1, 4 * high, width), BF16),
            vm((4 * high, width), BF16),
            vm((3, high, width), BF16),
            vm((high, width), F32),
            vm((ng - 1, high, width // ng), F32),
            vm((high, width // ng), BF16),
            vm((rounds, 2, 8, lanes), F32),
            vm((rounds, ng - 1, 8, lanes), F32),
            vm((rounds, ns - 1, 8, lanes), F32),
            dma((2 * rounds + 5,)),
            dma((rounds, 5)),
            dma((2, ng - 1)),
            dma((2, 2)),
            dma((steps, ng - 1)),
            dma((steps, ng - 1)),
            dma((steps, 2)),
            dma((steps, 2)),
            dma((steps, 2, 2 * nl, 2)),
            dma((steps, 2, 2 * nl, 2)),
            dma((4, nl - 1)),
            dma((4, 3)),
            dma((4, ng - 1)),
            dma((rounds, 2, ng - 1)),
            dma((rounds, 2, ns - 1)),
        ],
        compiler_params=pltpu.CompilerParams(
            collective_id=0, has_side_effects=True, vmem_limit_bytes=63 * 2**20
        ),
    )(lengths, chosen, ids, base, edits, targets, router, gate_weight, up_weight, down_weight)


def per_device(
    prompt_states, edit_offsets, targets, router, route_ids, chosen, lengths, w_gate, w_up, w_down
):
    seq = prompt_states.shape[2]
    rounds = route_ids.shape[0]
    top = route_ids.shape[4]
    experts = router.shape[1]
    cap = seq * top * 5 // (4 * experts)
    samplers = lax.axis_size("samp")
    groups = lax.axis_size("exp")
    block = -(-groups * cap // 16) * 16
    x, target, gate_side, up_side, weighted, advantage = step_call(
        lengths.reshape(rounds),
        chosen,
        route_ids[:, 0, 0],
        prompt_states[0, 0],
        edit_offsets[:, 0, 0],
        targets[:, 0, 0],
        router,
        w_gate[0],
        w_up[0],
        w_down[0],
        samplers,
        groups,
        block,
        cap,
    )
    return (
        dot_tn(x, gate_side).astype(BF16)[None],
        dot_tn(x, up_side).astype(BF16)[None],
        dot_tn(weighted, target).astype(BF16)[None],
        advantage[:, 0, :1].reshape(rounds, 1, 1),
    )


def solution(mesh):
    placed = (
        P("exp", "samp", None, None),
        P(None, "exp", "samp", None, None),
        P(None, "exp", "samp", None, None),
        P(),
        P(None, "exp", "samp", None, None),
        P(),
        P(None, "exp", "samp"),
        P(("samp", "exp"), None, None),
        P(("samp", "exp"), None, None),
        P(("samp", "exp"), None, None),
    )
    return jax.shard_map(
        per_device,
        mesh=mesh,
        in_specs=placed,
        out_specs=(
            P(("samp", "exp"), None, None),
            P(("samp", "exp"), None, None),
            P(("samp", "exp"), None, None),
            P(None, "exp", "samp"),
        ),
        check_vma=False,
    )
```

```python
import functools
import math

import jax
import jax.numpy as jnp
from jax import lax
from jax.experimental import pallas as pl
from jax.experimental.pallas import tpu as pltpu
from jax.sharding import PartitionSpec as P

F32 = jnp.float32
BF16 = jnp.bfloat16


def dot(a, b):
    return jnp.dot(a, b, preferred_element_type=F32)


def dot_tn(a, b):
    return lax.dot_general(a, b, (((0,), (0,)), ((), ())), preferred_element_type=F32)


def dot_nt(a, b):
    return lax.dot_general(a, b, (((1,), (1,)), ((), ())), preferred_element_type=F32)


MESH = pl.DeviceIdType.MESH
VMEM = pl.BlockSpec(memory_space=pltpu.VMEM)
ANY = pl.BlockSpec(memory_space=pl.ANY)


def greet(peers):
    for peer in peers:
        pl.semaphore_signal(pltpu.get_barrier_semaphore(), inc=1, device_id=peer, device_id_type=MESH)


def remote(src, dst, send, recv, peer):
    return pltpu.make_async_remote_copy(
        src_ref=src, dst_ref=dst, send_sem=send, recv_sem=recv, device_id=peer, device_id_type=MESH
    )


def add_all(terms):
    total = terms[0]
    for term in terms[1:]:
        total = total + term
    return total


def step_kernel(ns, ng, seq, top, block, cap, rounds, extra, chunks, shared, *refs):
    count = 2 * rounds
    length_ref, chosen_ref, ids_ref = refs[:3]
    base_hbm, edit_hbm, target_hbm, router_hbm, gate_hbm, up_hbm, down_hbm = refs[3:10]
    outs, adv_ref = refs[10:15], refs[15]
    rest = list(refs[16:])

    def take(n):
        taken = rest[:n]
        del rest[:n]
        return taken

    lands, alls, pairs, sends = take(count), take(count), take(count), take(1 if shared else 2)
    (
        gate_act, up_act, hid_act, code, codes, lines, place, router_ref, gate_w, up_w, down_w, result_ref, mixed,
        core_in, sub, rows_in, half, cols_in, final, vote, vote_z, vote_s, load_sem, store_sem, code_sem, line_sem,
        gs, gr, fs, bs, br, rs, rr, ss, sr, core_sem, plane_sem, z_sem, vote_zs, vote_ss,
    ) = rest
    width = base_hbm.shape[1]
    hidden = gate_w.shape[1]
    experts = ns * ng
    tokens = ng * seq
    rows = ns * block
    nl = ns // 4
    fan = 2 * nl
    tile = 256
    lanes = vote.shape[-1]
    me_s, me_g = lax.axis_index("samp"), lax.axis_index("exp")
    my_y, my_x, my_l = me_s // fan, lax.rem(me_s // nl, 2), lax.rem(me_s, nl)
    my_expert = me_s * ng + me_g

    def samp_at(y, x, l):
        return (y * 2 + x) * nl + l

    partners = [samp_at(1 - my_y, my_x, my_l), samp_at(my_y, 1 - my_x, my_l)]
    exp_peers = [(me_s, lax.rem(me_g + k, ng)) for k in range(1, ng)]
    samp_peers = [(lax.rem(me_s + k, ns), me_g) for k in range(1, ns)]
    mine = pl.ds(pl.multiple_of(me_g * seq, seq), seq)
    greet(exp_peers + samp_peers)

    def rows_of(d):
        return pl.ds(pl.multiple_of(d * block, block), block)

    loads = [
        pltpu.make_async_copy(source, target, load_sem.at[n])
        for n, (source, target) in enumerate(
            [(base_hbm, alls[0].at[mine, :width])]
            + [(target_hbm.at[0], alls[rounds].at[mine, :])]
            + [(edit_hbm.at[r - 1], alls[r].at[mine, :width]) for r in range(1, rounds)]
            + [(target_hbm.at[r], alls[rounds + r].at[mine, :]) for r in range(1, rounds)]
            + [(base_hbm, result_ref.at[block:, :])]
            + [(router_hbm, router_ref), (gate_hbm, gate_w), (up_hbm, up_w), (down_hbm, down_w)]
        )
    ]
    order = [0, rounds] + list(range(1, rounds)) + list(range(rounds + 1, count))
    for copy in loads:
        copy.start()

    row_p = lax.broadcasted_iota(jnp.int32, (experts, seq), 0).astype(F32)
    block_p = jnp.floor((row_p + 0.5) / ns)
    order_p = (row_p - block_p * ns) * ng + block_p
    row_m = lax.broadcasted_iota(jnp.int32, (extra, seq), 0)
    position = lax.broadcasted_iota(jnp.int32, (extra, seq), 1)
    row_e = lax.broadcasted_iota(jnp.int32, (seq, seq), 0)
    col_e = lax.broadcasted_iota(jnp.int32, (seq, seq), 1)
    eye = jnp.where(row_e == col_e, 1.0, 0.0).astype(BF16)
    upto = jnp.where(row_e <= col_e, 1.0, 0.0).astype(BF16)
    codes_own = []
    for r in range(rounds):
        ids = ids_ref[r]
        ids_f = ids.astype(F32)
        hit = add_all([jnp.where(ids_f[k : k + 1, :] == order_p, 1.0, 0.0) for k in range(top)])
        rank = dot(hit.astype(BF16), upto) - 1.0
        offset = (jnp.zeros((experts, seq), jnp.int32) + me_g * cap).astype(F32)
        codes_own.append(jnp.where(hit > 0.5, rank + offset, -1.0))
        length = jnp.zeros((extra, seq), jnp.int32) + length_ref[r]
        info = jnp.where(row_m == experts, position, 0)
        info = info + jnp.where((row_m == experts + 1) & (position < length), 1, 0)
        info = info + jnp.where(row_m == experts + 2, length, 0)
        info = info + jnp.where(row_m == experts + 3, 1, 0)
        for k in range(top):
            info = info + jnp.where(ids[k : k + 1, :] == row_m, 1, 0)
        alls[r][mine, width:] = dot_nt(eye, info.astype(F32).astype(BF16)).astype(BF16)
    line = jnp.concatenate(codes_own, axis=1)
    for g in range(ng):
        code[g] = line[g * ns : (g + 1) * ns, :]
    codes[0, me_g] = code[me_g]
    pl.semaphore_wait(pltpu.get_barrier_semaphore(), len(exp_peers + samp_peers))


    def z_piece(c, kind):
        i, lo, mid, hi, quota = chunks[c]
        return (alls[i], lo, hi) if kind == 0 else (pairs[i], mid - quota, mid + quota)

    def gather_copies(c, kind):
        tokens_ref, a, b = z_piece(c, kind)
        own = tokens_ref.at[mine, a:b]
        return [remote(own, own, gs.at[kind, c, k], gr.at[kind, c, k], p) for k, p in enumerate(exp_peers)]

    def ahead_copies(c):
        i, lo, mid, hi, quota = chunks[c]
        cuts = [(mid - quota, mid), (mid, mid + quota)] if quota else []
        return [
            remote(alls[i].at[mine, a:b], pairs[i].at[mine, a:b], bs.at[c, h], br.at[c, h], (partners[h], me_g))
            for h, (a, b) in enumerate(cuts)
        ]

    def relay_copies(c):
        i, lo, mid, hi, quota = chunks[c]
        return [
            remote(alls[i].at[:, a:b], pairs[i].at[:, a:b], rs.at[c, h], rr.at[c, h], (partners[h], me_g))
            for h, (a, b) in enumerate([(lo, mid - quota), (mid + quota, hi)])
            if a < b
        ]

    def start(copies):
        for copy in copies:
            copy.start()
        return copies

    def finish(copies):
        for copy in copies:
            copy.wait()

    ready = set()
    chain = ng == 4

    def z_start(c, kind):
        copies = gather_copies(c, kind)
        if chain:
            copies[1].start()
            pl.when(me_g != ng - 1)(copies[0].start)
            pl.when(me_g != 0)(copies[2].start)
        else:
            start(copies)

    def forward_copy(c, kind, owner, there):
        tokens_ref, a, b = z_piece(c, kind)
        piece = tokens_ref.at[owner * seq : (owner + 1) * seq, a:b]
        return remote(piece, piece, fs.at[kind, c], gr.at[kind, c, (there - owner) % ng - 1], (me_s, there))

    def z_forward(c, kind):
        if chain:
            gather_copies(c, kind)[1].wait_recv()
            pl.when(me_g == 1)(forward_copy(c, kind, 3, 0).start)
            pl.when(me_g == 2)(forward_copy(c, kind, 0, 3).start)

    def z_finish(c, kind):
        copies = gather_copies(c, kind)
        if chain:
            copies[1].wait_send()
            copies[0].wait_recv()
            copies[2].wait_recv()
            pl.when(me_g != ng - 1)(copies[0].wait_send)
            pl.when(me_g != 0)(copies[2].wait_send)
            pl.when((me_g == 1) | (me_g == 2))(forward_copy(c, kind, 0, 3).wait_send)
        else:
            finish(copies)

    def gather(c):
        if c < len(chunks):
            i = chunks[c][0]
            if i not in ready:
                ready.add(i)
                loads[order.index(i)].wait()
            start(ahead_copies(c))
            z_start(c, 0)

    def forward(c):
        if c < len(chunks):
            z_forward(c, 0)
            if chunks[c][4]:
                finish(ahead_copies(c))
                z_start(c, 1)

    def relay(c):
        z_finish(c, 0)
        start(relay_copies(c))
        gather(c + 2)
        forward(c + 1)
        if chunks[c][4]:
            z_forward(c, 1)

    def dest_of(h, k):
        l = lax.rem(my_l + lax.rem(k, nl), nl)
        if h == 0:
            return samp_at(my_y, lax.rem(my_x + k // nl, 2), l)
        return samp_at(lax.rem(my_y + k // nl, 2), my_x, l)

    def cols_at(c, h):
        i, lo, mid, hi, quota = chunks[c]
        return (lo, mid) if h == 0 else (mid, hi)

    def buffer_of(c):
        return sends[0 if shared else chunks[c][0] // rounds]

    def slot_copy(c, h, k, b):
        i = chunks[c][0]
        a, e = cols_at(c, h)
        home = me_s if b == 0 else partners[h]
        return remote(
            buffer_of(c).at[rows_of(b * fan + k), a:e],
            lands[i].at[rows_of(home), a:e],
            ss.at[c, h, k, b],
            sr.at[c, h, k, b],
            (dest_of(h, k), me_g),
        )

    done = set()

    def landed(c):
        if c in done:
            return
        done.add(c)

        def step(k, carry):
            for h in range(2):
                for b in range(2):
                    slot_copy(c, h, k, b).wait()
            return carry

        lax.fori_loop(1, fan, step, 0)

    def scatter(c):
        i = chunks[c][0]
        finish(relay_copies(c))
        if chunks[c][4]:
            z_finish(c, 1)
        for p in range(c):
            if (shared or chunks[p][0] // rounds == i // rounds) and chunks[p][1] == chunks[c][1]:
                landed(p)
        for h in range(2):
            a, e = cols_at(c, h)
            for b in range(2):
                tokens_ref = alls[i] if b == 0 else pairs[i]
                placed = dot(place[i % rounds, h, b], tokens_ref[:, a:e]).astype(BF16)
                buffer_of(c)[(b * fan + 1) * block : (b + 1) * fan * block, a:e] = placed[block:]
                home = me_s if b == 0 else partners[h]
                lands[i][rows_of(home), a:e] = placed[:block]

                def step(n, carry, h=h, b=b):
                    slot_copy(c, h, fan - n, b).start()
                    return carry

                lax.fori_loop(1, fan, step, 0)

    code_copies = start(
        [
            remote(code.at[peer[1]], codes.at[0, me_g], code_sem.at[0, k], code_sem.at[1, k], peer)
            for k, peer in enumerate(exp_peers)
        ]
    )
    gather(0)
    gather(1)
    forward(0)
    finish(code_copies)
    line_copies = start(
        [
            remote(codes.at[0], codes.at[1 + h], line_sem.at[0, h], line_sem.at[1, h], (partners[h], me_g))
            for h in range(2)
        ]
    )
    relay(0)
    finish(line_copies)
    slots = lax.broadcasted_iota(jnp.int32, (block, tokens), 0).astype(F32)
    for r in range(rounds):
        for who in range(3):
            lines[r, who] = jnp.concatenate(
                [codes[who, g][:, r * seq : (r + 1) * seq] for g in range(ng)], axis=1
            )
        for h in range(2):
            for b in range(2):
                for k in range(fan):
                    line = lines[r, 0 if b == 0 else 1 + h, pl.ds(dest_of(h, k), 1), :]
                    hit = jnp.where(line == slots, 1.0, 0.0)
                    place[r, h, b, k * block : (k + 1) * block, :] = hit.astype(BF16)

    row_i = lax.broadcasted_iota(jnp.int32, (rows, 1), 0)
    row_samp = add_all([jnp.where(row_i >= d * block, 1, 0) for d in range(1, ns)])
    row_slot = row_i - row_samp * block
    row_group = add_all([jnp.where(row_slot >= g * cap, 1, 0) for g in range(1, ng)])
    lane_v = lax.broadcasted_iota(jnp.int32, (rows, lanes), 1)
    repair_hot = row_samp * ng + row_group == lane_v
    scale = 1.0 / math.sqrt(width)

    def stores(r, n):
        source = (lands[r].at[:, :width], lands[rounds + r], gate_act.at[r], up_act.at[r], hid_act.at[r])[n]
        target = outs[n].at[r * rows : (r + 1) * rows, :]
        return pltpu.make_async_copy(source, target, store_sem.at[r, n])

    def project(r):
        def step(n, carry):
            cols = pl.ds(pl.multiple_of(n * tile, tile), tile)
            pre_gate = dot(lands[r][:, :width], gate_w[:, cols])
            pre_up = dot(lands[r][:, :width], up_w[:, cols])
            sg = jax.nn.sigmoid(pre_gate)
            silu = pre_gate * sg
            hid_act[r, :, cols] = (silu * pre_up).astype(BF16)
            gate_act[r, :, cols] = (pre_up * sg * (1.0 + pre_gate * (1.0 - sg))).astype(BF16)
            up_act[r, :, cols] = silu.astype(BF16)
            return carry

        lax.fori_loop(0, hidden // tile, step, 0)

    def row_info(r):
        first = (experts // 128) * 128
        last = lands[r][:, width + first : width + first + 128].astype(F32)
        lane_i = lax.broadcasted_iota(jnp.int32, (rows, 128), 1)
        return [
            jnp.sum(jnp.where(lane_i == experts - first + n, last, 0.0), axis=1, keepdims=True) for n in range(4)
        ]

    def gates(r, used):
        lane = lax.broadcasted_iota(jnp.int32, (rows, experts), 1)
        mask = lands[r][:, width : width + experts].astype(F32) > 0.5
        sig = jnp.where(mask, jax.nn.sigmoid(dot_nt(lands[r][:, :width], router_ref[...])), 0.0)
        total = jnp.where(used, jnp.sum(sig, axis=1, keepdims=True), 1.0)
        share = jnp.sum(jnp.where(lane == my_expert, sig, 0.0), axis=1, keepdims=True)
        return (share / total).astype(BF16).astype(F32)

    def backward(r):
        def step(n, score):
            cols = pl.ds(pl.multiple_of(n * tile, tile), tile)
            back = dot_nt(lands[rounds + r][...], down_w[cols, :])
            gate_act[r, :, cols] = (gate_act[r, :, cols].astype(F32) * back).astype(BF16)
            up_act[r, :, cols] = (up_act[r, :, cols].astype(F32) * back).astype(BF16)
            return score + jnp.sum(hid_act[r, :, cols].astype(F32) * back, axis=1, keepdims=True)

        return lax.fori_loop(0, hidden // tile, step, jnp.zeros((rows, 1), F32))

    def own_reward(r):
        x = alls[r][mine, :width].astype(F32)
        if r > 0:
            x = (x + mixed[mine, :].astype(F32)).astype(BF16).astype(F32)
        score = jnp.sum(x * alls[rounds + r][mine, :].astype(F32), axis=1, keepdims=True) * scale
        place_t = lax.broadcasted_iota(jnp.int32, (seq, 1), 0)
        score = jnp.where(place_t < length_ref[r], score, 0.0)
        length = (jnp.zeros((1, 1), jnp.int32) + length_ref[r]).astype(F32)
        return jnp.sum(score, axis=0, keepdims=True) / length

    def vote_copies(r, phase):
        if phase == 0:
            return [
                remote(vote.at[r, 0], vote_z.at[r, k], vote_zs.at[r, 0, k], vote_zs.at[r, 1, k], peer)
                for k, peer in enumerate(exp_peers)
            ]
        return [
            remote(vote.at[r, 1], vote_s.at[r, k], vote_ss.at[r, 0, k], vote_ss.at[r, 1, k], peer)
            for k, peer in enumerate(samp_peers)
        ]

    def vote_open(r, score, gate, info, own):
        used = info[3] > 0.5
        row_score = gate * info[1] * (score * scale) / jnp.where(used, info[2], 1.0)
        lane = lax.broadcasted_iota(jnp.int32, (8, lanes), 1)
        parts = jnp.sum(jnp.where(repair_hot, row_score, 0.0), axis=0, keepdims=True)
        vote[r, 0] = jnp.where(lane == my_expert, own, 0.0) + parts
        start(vote_copies(r, 0))

    def vote_pass(r):
        total = vote[r, 0]
        for k, copy in enumerate(vote_copies(r, 0)):
            copy.wait()
            total = total + vote_z[r, k]
        vote[r, 1] = total
        start(vote_copies(r, 1))

    def vote_close(r):
        total = vote[r, 1]
        for k, copy in enumerate(vote_copies(r, 1)):
            copy.wait()
            total = total + vote_s[r, k]
        lane = lax.broadcasted_iota(jnp.int32, (8, lanes), 1).astype(F32)
        group = lane - jnp.floor((lane + 0.5) / ng) * ng
        mean = jnp.zeros((8, lanes), F32)
        for g in range(ng):
            member = (group == g) & (lane < experts)
            sums = jnp.sum(jnp.where(member, total, 0.0), axis=1, keepdims=True)
            mean = mean + jnp.where(member, sums / ns, 0.0)
        advantage = total - mean
        lane_i = lax.broadcasted_iota(jnp.int32, (8, lanes), 1)
        row = lax.broadcasted_iota(jnp.int32, (8, lanes), 0)
        adv_ref[r] = jnp.sum(jnp.where((lane_i == my_expert) & (row == 0), advantage, 0.0))
        return advantage

    def weigh(r, advantage, gate, info):
        row_adv = jnp.sum(jnp.where(repair_hot, advantage[:1, :], 0.0), axis=1, keepdims=True)
        coef = (row_adv * info[1] * gate).astype(BF16).astype(F32)
        for act in (gate_act, up_act, hid_act):
            act[r] = (act[r].astype(F32) * coef).astype(BF16)

    high = rows_in.shape[1]
    wide = width // ng
    tall = 4 * high
    my_yx = my_y * 2 + my_x
    my_part = my_l * 4 + my_yx

    def high_of(d):
        return pl.ds(pl.multiple_of(d * high, high), high)

    def tall_of(l):
        return pl.ds(pl.multiple_of(l * tall, tall), tall)

    def cols_of(g):
        return pl.ds(pl.multiple_of(g * wide, wide), wide)

    core_peers = [lax.rem(my_l + n, nl) for n in range(1, nl)]
    plane_peers = [lax.rem(my_yx + n, 4) for n in range(1, 4)]

    part = alls[0].at[:, :width]

    def mix_copies(phase):
        if phase == 0:
            pieces = [
                (part.at[tall_of(l), :], core_in.at[n], core_sem, n, (my_yx * nl + l, me_g))
                for n, l in enumerate(core_peers)
            ]
        elif phase == 1:
            pieces = [
                (sub.at[high_of(p), :], rows_in.at[n], plane_sem, n, (p * nl + my_l, me_g))
                for n, p in enumerate(plane_peers)
            ]
        elif phase == 2:
            pieces = [
                (half.at[:, cols_of(peer[1])], cols_in.at[n], z_sem, n, peer) for n, peer in enumerate(exp_peers)
            ]
        elif phase == 3:
            there = mixed.at[high_of(my_part), cols_of(me_g)]
            pieces = [(final, there, z_sem, n, peer) for n, peer in enumerate(exp_peers)]
        elif phase == 4:
            there = mixed.at[high_of(my_part), :]
            pieces = [(there, there, plane_sem, n, (p * nl + my_l, me_g)) for n, p in enumerate(plane_peers)]
        else:
            there = mixed.at[tall_of(my_l), :]
            pieces = [(there, there, core_sem, n, (my_yx * nl + l, me_g)) for n, l in enumerate(core_peers)]
        late = 2 if phase > 2 else 0
        return [remote(a, b, sem.at[late, n], sem.at[late + 1, n], peer) for a, b, sem, n, peer in pieces]

    def mix_sum_core():
        finish(mix_copies(0))
        total = part[tall_of(my_l), :].astype(F32)
        for n in range(nl - 1):
            total = total + core_in[n].astype(F32)
        sub[...] = total.astype(BF16)
        start(mix_copies(1))

    def mix_sum_plane():
        finish(mix_copies(1))
        total = sub[high_of(my_yx), :].astype(F32)
        for n in range(3):
            total = total + rows_in[n].astype(F32)
        half[...] = total
        start(mix_copies(2))

    def mix_sum_z():
        finish(mix_copies(2))
        total = half[:, cols_of(me_g)]
        for n in range(ng - 1):
            total = total + cols_in[n]
        final[...] = total.astype(BF16)
        mixed[high_of(my_part), cols_of(me_g)] = final[...]
        start(mix_copies(3))

    def step(c):
        if c < len(chunks):
            relay(c)
        scatter(c - 1)

    for c in range(1, 6):
        step(c)
    finish(loads[count:])
    for c in range(4):
        landed(c)
    stores(0, 0).start()
    project(0)
    step(6)

    info_0 = row_info(0)
    used_0 = info_0[3] > 0.5
    gate_0 = gates(0, used_0)
    slot = lax.broadcasted_iota(jnp.int32, (block, 1), 0)
    slot_group = add_all([jnp.where(slot >= g * cap, 1, 0) for g in range(1, ng)])
    choice = add_all([jnp.where(slot_group == g, chosen_ref[0, g], 0) for g in range(ng)])
    hidden_sel = jnp.zeros((block, hidden), F32)
    gate_sel = jnp.zeros((block, 1), F32)
    spot_sel = jnp.zeros((block, 1), F32)
    spot = jnp.where(used_0, info_0[0], -float(tokens))
    for d in range(ns):
        keep = choice == d
        at = slice(d * block, (d + 1) * block)
        hidden_sel = hidden_sel + jnp.where(keep, hid_act[0, at, :].astype(F32), 0.0)
        gate_sel = gate_sel + jnp.where(keep, gate_0[at], 0.0)
        spot_sel = spot_sel + jnp.where(keep, spot[at], 0.0)
    spot_sel = spot_sel + (slot_group * seq).astype(F32)
    result_ref[:block, :] = dot(hidden_sel.astype(BF16), down_w[...]).astype(BF16)
    token = lax.broadcasted_iota(jnp.int32, (block, tokens), 1).astype(F32)
    spread = jnp.where(spot_sel == token, gate_sel, 0.0)
    lead = lax.broadcasted_iota(jnp.int32, (seq, tokens), 0) + me_g * seq
    at_token = lax.broadcasted_iota(jnp.int32, (seq, tokens), 1)
    best = jnp.zeros((seq, tokens), jnp.int32) + chosen_ref[0, me_g]
    own_hot = jnp.where((lead == at_token) & (best == me_s), 1.0, 0.0)
    combine = jnp.concatenate([spread, own_hot], axis=0).astype(BF16)
    own_0 = own_reward(0)
    part[...] = dot_tn(combine, result_ref[...]).astype(BF16)
    start(mix_copies(0))
    step(7)
    mix_sum_core()
    step(8)
    step(9)
    mix_sum_plane()
    step(10)
    mix_sum_z()
    step(11)
    for c in range(4, 8):
        landed(c)
    stores(0, 1).start()
    score_0 = backward(0)
    vote_open(0, score_0, gate_0, info_0, own_0)
    finish(mix_copies(3))
    start(mix_copies(4))
    step(12)
    step(13)
    finish(mix_copies(4))
    start(mix_copies(5))
    vote_pass(0)
    step(14)
    finish(mix_copies(5))
    for c in range(8, 12):
        landed(c)

    info_1 = row_info(1)
    used_1 = info_1[3] > 0.5
    spot_1 = jnp.where(used_1, info_1[0] + (row_group * seq).astype(F32), -1.0)
    token_r = lax.broadcasted_iota(jnp.int32, (rows, tokens), 1).astype(F32)
    lift = jnp.where(spot_1 == token_r, 1.0, 0.0).astype(BF16)
    for n in range(0, width, 2 * tile):
        cols = slice(n, n + 2 * tile)
        lifted = dot(lift, mixed[:, cols]) + lands[1][:, cols].astype(F32)
        lands[1][:, cols] = lifted.astype(BF16)
    step(15)
    stores(1, 0).start()
    project(1)
    step(16)
    gate_1 = gates(1, used_1)
    weigh(0, vote_close(0), gate_0, info_0)
    for n in range(2, 5):
        stores(0, n).start()
    for c in range(12, 16):
        landed(c)
    stores(1, 1).start()
    vote_open(1, backward(1), gate_1, info_1, own_reward(1))
    vote_pass(1)
    weigh(1, vote_close(1), gate_1, info_1)
    for n in range(2, 5):
        stores(1, n).start()
    for r in range(rounds):
        for n in range(5):
            stores(r, n).wait()


def step_call(
    lengths, chosen, ids, base, edits, targets, router, gate_weight, up_weight, down_weight, ns, ng, block, cap
):
    rounds, top, seq = ids.shape
    experts, width = router.shape
    hidden = gate_weight.shape[1]
    extra = -(-(experts + 4) // 128) * 128
    lanes = -(-experts // 128) * 128
    rows, tokens = ns * block, ng * seq
    full = width + extra
    piece = width // 16
    chunks = []
    for r in range(rounds):
        for i in (r, rounds + r):
            for n in range(4):
                at = n * 4 * piece
                end = full if i < rounds and n == 3 else at + 4 * piece
                chunks.append((i, at, at + 2 * piece, end, piece if len(chunks) >= 8 else 0))
    steps = len(chunks)
    widths = [full] * rounds + [width] * rounds
    smem = pl.BlockSpec(memory_space=pltpu.SMEM)
    nl = ns // 4
    high = tokens // ns
    shared = rows * tokens > 640 * 256
    dma = pltpu.SemaphoreType.DMA
    vm = pltpu.VMEM
    return pl.pallas_call(
        functools.partial(step_kernel, ns, ng, seq, top, block, cap, rounds, extra, chunks, shared),
        out_shape=[jax.ShapeDtypeStruct((rounds * rows, width), BF16)] * 2
        + [jax.ShapeDtypeStruct((rounds * rows, hidden), BF16)] * 3
        + [jax.ShapeDtypeStruct((rounds,), F32)],
        in_specs=[smem, smem, VMEM] + [ANY] * 7,
        out_specs=[ANY] * 5 + [smem],
        scratch_shapes=[vm((rows, w), BF16) for w in widths]
        + [vm((tokens, w), BF16) for w in widths] * 2
        + [vm((rows, full), BF16)]
        + ([] if shared else [vm((rows, width), BF16)])
        + [vm((rounds, rows, hidden), BF16)] * 3
        + [
            vm((ng, ns, rounds * seq), F32),
            vm((3, ng, ns, rounds * seq), F32),
            vm((rounds, 3, ns, tokens), F32),
            vm((rounds, 2, 2, 2 * nl * block, tokens), BF16),
            vm(router.shape, BF16),
            vm(gate_weight.shape, BF16),
            vm(up_weight.shape, BF16),
            vm(down_weight.shape, BF16),
            vm((block + seq, width), BF16),
            vm((tokens, width), BF16),
            vm((nl - 1, 4 * high, width), BF16),
            vm((4 * high, width), BF16),
            vm((3, high, width), BF16),
            vm((high, width), F32),
            vm((ng - 1, high, width // ng), F32),
            vm((high, width // ng), BF16),
            vm((rounds, 2, 8, lanes), F32),
            vm((rounds, ng - 1, 8, lanes), F32),
            vm((rounds, ns - 1, 8, lanes), F32),
            dma((2 * rounds + 5,)),
            dma((rounds, 5)),
            dma((2, ng - 1)),
            dma((2, 2)),
            dma((2, steps, ng - 1)),
            dma((2, steps, ng - 1)),
            dma((2, steps)),
            dma((steps, 2)),
            dma((steps, 2)),
            dma((steps, 2)),
            dma((steps, 2)),
            dma((steps, 2, 2 * nl, 2)),
            dma((steps, 2, 2 * nl, 2)),
            dma((4, nl - 1)),
            dma((4, 3)),
            dma((4, ng - 1)),
            dma((rounds, 2, ng - 1)),
            dma((rounds, 2, ns - 1)),
        ],
        compiler_params=pltpu.CompilerParams(
            collective_id=0, has_side_effects=True, vmem_limit_bytes=63 * 2**20
        ),
    )(lengths, chosen, ids, base, edits, targets, router, gate_weight, up_weight, down_weight)


def per_device(
    prompt_states, edit_offsets, targets, router, route_ids, chosen, lengths, w_gate, w_up, w_down
):
    seq = prompt_states.shape[2]
    rounds = route_ids.shape[0]
    top = route_ids.shape[4]
    experts = router.shape[1]
    cap = seq * top * 5 // (4 * experts)
    samplers = lax.axis_size("samp")
    groups = lax.axis_size("exp")
    block = -(-groups * cap // 16) * 16
    x, target, gate_side, up_side, weighted, advantage = step_call(
        lengths.reshape(rounds),
        chosen,
        route_ids[:, 0, 0].swapaxes(1, 2),
        prompt_states[0, 0],
        edit_offsets[:, 0, 0],
        targets[:, 0, 0],
        router.T,
        w_gate[0],
        w_up[0],
        w_down[0],
        samplers,
        groups,
        block,
        cap,
    )
    return (
        dot_tn(x, gate_side).astype(BF16)[None],
        dot_tn(x, up_side).astype(BF16)[None],
        dot_tn(weighted, target).astype(BF16)[None],
        advantage.reshape(rounds, 1, 1),
    )


def solution(mesh):
    placed = (
        P("exp", "samp", None, None),
        P(None, "exp", "samp", None, None),
        P(None, "exp", "samp", None, None),
        P(),
        P(None, "exp", "samp", None, None),
        P(),
        P(None, "exp", "samp"),
        P(("samp", "exp"), None, None),
        P(("samp", "exp"), None, None),
        P(("samp", "exp"), None, None),
    )
    return jax.shard_map(
        per_device,
        mesh=mesh,
        in_specs=placed,
        out_specs=(
            P(("samp", "exp"), None, None),
            P(("samp", "exp"), None, None),
            P(("samp", "exp"), None, None),
            P(None, "exp", "samp"),
        ),
        check_vma=False,
    )
```

```python
import functools
import math

import jax
import jax.numpy as jnp
from jax import lax
from jax.experimental import pallas as pl
from jax.experimental.pallas import tpu as pltpu
from jax.sharding import PartitionSpec as P

F32 = jnp.float32
BF16 = jnp.bfloat16


def dot(a, b):
    return jnp.dot(a, b, preferred_element_type=F32)


def dot_tn(a, b):
    return lax.dot_general(a, b, (((0,), (0,)), ((), ())), preferred_element_type=F32)


def dot_nt(a, b):
    return lax.dot_general(a, b, (((1,), (1,)), ((), ())), preferred_element_type=F32)


MESH = pl.DeviceIdType.MESH
VMEM = pl.BlockSpec(memory_space=pltpu.VMEM)
ANY = pl.BlockSpec(memory_space=pl.ANY)


def greet(peers):
    for peer in peers:
        pl.semaphore_signal(pltpu.get_barrier_semaphore(), inc=1, device_id=peer, device_id_type=MESH)


def remote(src, dst, send, recv, peer):
    return pltpu.make_async_remote_copy(
        src_ref=src, dst_ref=dst, send_sem=send, recv_sem=recv, device_id=peer, device_id_type=MESH
    )


def add_all(terms):
    total = terms[0]
    for term in terms[1:]:
        total = total + term
    return total


def step_kernel(ns, ng, seq, top, block, cap, rounds, extra, chunks, shared, *refs):
    count = 2 * rounds
    length_ref, chosen_ref, ids_ref = refs[:3]
    base_hbm, edit_hbm, target_hbm, router_hbm, gate_hbm, up_hbm, down_hbm = refs[3:10]
    outs, adv_ref = refs[10:15], refs[15]
    rest = list(refs[16:])

    def take(n):
        taken = rest[:n]
        del rest[:n]
        return taken

    lands, alls, pairs, sends = take(count), take(count), take(count), take(1 if shared else 2)
    backs = take(0 if shared else 1)
    (
        gate_act, up_act, hid_act, code, codes, lines, place, router_ref, gate_w, up_w, down_w, result_ref, mixed,
        core_in, sub, rows_in, half, cols_in, vote, vote_z, vote_s, load_sem, store_sem, code_sem, line_sem,
        gs, gr, fs, bs, br, rs, rr, ss, sr, core_sem, plane_sem, z_sem, vote_zs, vote_ss,
    ) = rest
    width = base_hbm.shape[1]
    hidden = gate_w.shape[1]
    experts = ns * ng
    tokens = ng * seq
    rows = ns * block
    nl = ns // 4
    fan = 2 * nl
    tile = 256
    lanes = vote.shape[-1]
    me_s, me_g = lax.axis_index("samp"), lax.axis_index("exp")
    my_y, my_x, my_l = me_s // fan, lax.rem(me_s // nl, 2), lax.rem(me_s, nl)
    my_expert = me_s * ng + me_g

    def samp_at(y, x, l):
        return (y * 2 + x) * nl + l

    partners = [samp_at(1 - my_y, my_x, my_l), samp_at(my_y, 1 - my_x, my_l)]
    exp_peers = [(me_s, lax.rem(me_g + k, ng)) for k in range(1, ng)]
    samp_peers = [(lax.rem(me_s + k, ns), me_g) for k in range(1, ns)]
    mine = pl.ds(pl.multiple_of(me_g * seq, seq), seq)
    greet(exp_peers + samp_peers)

    def rows_of(d):
        return pl.ds(pl.multiple_of(d * block, block), block)

    loads = [
        pltpu.make_async_copy(source, target, load_sem.at[n])
        for n, (source, target) in enumerate(
            [(base_hbm, alls[0].at[mine, :width])]
            + [(target_hbm.at[0], alls[rounds].at[mine, :])]
            + [(edit_hbm.at[r - 1], alls[r].at[mine, :width]) for r in range(1, rounds)]
            + [(target_hbm.at[r], alls[rounds + r].at[mine, :]) for r in range(1, rounds)]
            + [(base_hbm, result_ref.at[block:, :])]
            + [(router_hbm, router_ref), (gate_hbm, gate_w), (up_hbm, up_w), (down_hbm, down_w)]
        )
    ]
    order = [0, rounds] + list(range(1, rounds)) + list(range(rounds + 1, count))
    for copy in loads:
        copy.start()

    row_p = lax.broadcasted_iota(jnp.int32, (experts, seq), 0).astype(F32)
    block_p = jnp.floor((row_p + 0.5) / ns)
    order_p = (row_p - block_p * ns) * ng + block_p
    row_m = lax.broadcasted_iota(jnp.int32, (extra, seq), 0)
    position = lax.broadcasted_iota(jnp.int32, (extra, seq), 1)
    row_e = lax.broadcasted_iota(jnp.int32, (seq, seq), 0)
    col_e = lax.broadcasted_iota(jnp.int32, (seq, seq), 1)
    eye = jnp.where(row_e == col_e, 1.0, 0.0).astype(BF16)
    upto = jnp.where(row_e <= col_e, 1.0, 0.0).astype(BF16)
    codes_own = []
    for r in range(rounds):
        ids = ids_ref[r]
        ids_f = ids.astype(F32)
        hit = add_all([jnp.where(ids_f[k : k + 1, :] == order_p, 1.0, 0.0) for k in range(top)])
        rank = dot(hit.astype(BF16), upto) - 1.0
        offset = (jnp.zeros((experts, seq), jnp.int32) + me_g * cap).astype(F32)
        codes_own.append(jnp.where(hit > 0.5, rank + offset, -1.0))
        length = jnp.zeros((extra, seq), jnp.int32) + length_ref[r]
        info = jnp.where(row_m == experts, position, 0)
        info = info + jnp.where((row_m == experts + 1) & (position < length), 1, 0)
        info = info + jnp.where(row_m == experts + 2, length, 0)
        info = info + jnp.where(row_m == experts + 3, 1, 0)
        for k in range(top):
            info = info + jnp.where(ids[k : k + 1, :] == row_m, 1, 0)
        alls[r][mine, width:] = dot_nt(eye, info.astype(F32).astype(BF16)).astype(BF16)
    line = jnp.concatenate(codes_own, axis=1)
    for g in range(ng):
        code[g] = line[g * ns : (g + 1) * ns, :]
    codes[0, me_g] = code[me_g]
    pl.semaphore_wait(pltpu.get_barrier_semaphore(), len(exp_peers + samp_peers))


    def z_piece(c, kind):
        i, lo, mid, hi, quota = chunks[c]
        return (alls[i], lo, hi) if kind == 0 else (pairs[i], mid - quota, mid + quota)

    def gather_copies(c, kind):
        tokens_ref, a, b = z_piece(c, kind)
        own = tokens_ref.at[mine, a:b]
        return [remote(own, own, gs.at[kind, c, k], gr.at[kind, c, k], p) for k, p in enumerate(exp_peers)]

    def ahead_copies(c):
        i, lo, mid, hi, quota = chunks[c]
        cuts = [(mid - quota, mid), (mid, mid + quota)] if quota else []
        return [
            remote(alls[i].at[mine, a:b], pairs[i].at[mine, a:b], bs.at[c, h], br.at[c, h], (partners[h], me_g))
            for h, (a, b) in enumerate(cuts)
        ]

    def relay_copies(c):
        i, lo, mid, hi, quota = chunks[c]
        return [
            remote(alls[i].at[:, a:b], pairs[i].at[:, a:b], rs.at[c, h], rr.at[c, h], (partners[h], me_g))
            for h, (a, b) in enumerate([(lo, mid - quota), (mid + quota, hi)])
            if a < b
        ]

    def start(copies):
        for copy in copies:
            copy.start()
        return copies

    def finish(copies):
        for copy in copies:
            copy.wait()

    ready = set()
    chain = ng == 4

    def z_start(c, kind):
        copies = gather_copies(c, kind)
        if chain:
            copies[1].start()
            pl.when(me_g != ng - 1)(copies[0].start)
            pl.when(me_g != 0)(copies[2].start)
        else:
            start(copies)

    def forward_copy(c, kind, owner, there):
        tokens_ref, a, b = z_piece(c, kind)
        piece = tokens_ref.at[owner * seq : (owner + 1) * seq, a:b]
        return remote(piece, piece, fs.at[kind, c], gr.at[kind, c, (there - owner) % ng - 1], (me_s, there))

    def z_forward(c, kind):
        if chain:
            gather_copies(c, kind)[1].wait_recv()
            pl.when(me_g == 1)(forward_copy(c, kind, 3, 0).start)
            pl.when(me_g == 2)(forward_copy(c, kind, 0, 3).start)

    def z_finish(c, kind):
        copies = gather_copies(c, kind)
        if chain:
            copies[1].wait_send()
            copies[0].wait_recv()
            copies[2].wait_recv()
            pl.when(me_g != ng - 1)(copies[0].wait_send)
            pl.when(me_g != 0)(copies[2].wait_send)
            pl.when((me_g == 1) | (me_g == 2))(forward_copy(c, kind, 0, 3).wait_send)
        else:
            finish(copies)

    def gather(c):
        if c < len(chunks):
            i = chunks[c][0]
            if i not in ready:
                ready.add(i)
                loads[order.index(i)].wait()
            start(ahead_copies(c))
            z_start(c, 0)

    def forward(c):
        if c < len(chunks):
            z_forward(c, 0)
            if chunks[c][4]:
                finish(ahead_copies(c))
                z_start(c, 1)

    def relay(c):
        z_finish(c, 0)
        start(relay_copies(c))
        gather(c + 2)
        forward(c + 1)
        if chunks[c][4]:
            z_forward(c, 1)

    def dest_of(h, k):
        l = lax.rem(my_l + lax.rem(k, nl), nl)
        if h == 0:
            return samp_at(my_y, lax.rem(my_x + k // nl, 2), l)
        return samp_at(lax.rem(my_y + k // nl, 2), my_x, l)

    def cols_at(c, h):
        i, lo, mid, hi, quota = chunks[c]
        return (lo, mid) if h == 0 else (mid, hi)

    def buffer_of(c):
        return sends[0 if shared else chunks[c][0] // rounds]

    def slot_copy(c, h, k, b):
        i = chunks[c][0]
        a, e = cols_at(c, h)
        home = me_s if b == 0 else partners[h]
        return remote(
            buffer_of(c).at[rows_of(b * fan + k), a:e],
            lands[i].at[rows_of(home), a:e],
            ss.at[c, h, k, b],
            sr.at[c, h, k, b],
            (dest_of(h, k), me_g),
        )

    done = set()

    def landed(c):
        if c in done:
            return
        done.add(c)

        def step(k, carry):
            for h in range(2):
                for b in range(2):
                    slot_copy(c, h, k, b).wait()
            return carry

        lax.fori_loop(1, fan, step, 0)

    def scatter(c):
        i = chunks[c][0]
        finish(relay_copies(c))
        if chunks[c][4]:
            z_finish(c, 1)
        for p in range(c):
            if (shared or chunks[p][0] // rounds == i // rounds) and chunks[p][1] == chunks[c][1]:
                landed(p)
        for h in range(2):
            a, e = cols_at(c, h)
            for b in range(2):
                tokens_ref = alls[i] if b == 0 else pairs[i]
                placed = dot(place[i % rounds, h, b], tokens_ref[:, a:e]).astype(BF16)
                buffer_of(c)[(b * fan + 1) * block : (b + 1) * fan * block, a:e] = placed[block:]
                home = me_s if b == 0 else partners[h]
                lands[i][rows_of(home), a:e] = placed[:block]

                def step(n, carry, h=h, b=b):
                    slot_copy(c, h, fan - n, b).start()
                    return carry

                lax.fori_loop(1, fan, step, 0)

    code_copies = start(
        [
            remote(code.at[peer[1]], codes.at[0, me_g], code_sem.at[0, k], code_sem.at[1, k], peer)
            for k, peer in enumerate(exp_peers)
        ]
    )
    gather(0)
    gather(1)
    forward(0)
    finish(code_copies)
    line_copies = start(
        [
            remote(codes.at[0], codes.at[1 + h], line_sem.at[0, h], line_sem.at[1, h], (partners[h], me_g))
            for h in range(2)
        ]
    )
    relay(0)
    finish(line_copies)
    slots = lax.broadcasted_iota(jnp.int32, (block, tokens), 0).astype(F32)
    for r in range(rounds):
        for who in range(3):
            lines[r, who] = jnp.concatenate(
                [codes[who, g][:, r * seq : (r + 1) * seq] for g in range(ng)], axis=1
            )
        for h in range(2):
            for b in range(2):
                for k in range(fan):
                    line = lines[r, 0 if b == 0 else 1 + h, pl.ds(dest_of(h, k), 1), :]
                    hit = jnp.where(line == slots, 1.0, 0.0)
                    place[r, h, b, k * block : (k + 1) * block, :] = hit.astype(BF16)

    row_i = lax.broadcasted_iota(jnp.int32, (rows, 1), 0)
    row_samp = add_all([jnp.where(row_i >= d * block, 1, 0) for d in range(1, ns)])
    row_slot = row_i - row_samp * block
    row_group = add_all([jnp.where(row_slot >= g * cap, 1, 0) for g in range(1, ng)])
    lane_v = lax.broadcasted_iota(jnp.int32, (rows, lanes), 1)
    repair_hot = row_samp * ng + row_group == lane_v
    scale = 1.0 / math.sqrt(width)

    def stores(r, n):
        source = (lands[r].at[:, :width], lands[rounds + r], gate_act.at[r], up_act.at[r], hid_act.at[r])[n]
        target = outs[n].at[r * rows : (r + 1) * rows, :]
        return pltpu.make_async_copy(source, target, store_sem.at[r, n])

    def project(r):
        def step(n, carry):
            cols = pl.ds(pl.multiple_of(n * tile, tile), tile)
            pre_gate = dot(lands[r][:, :width], gate_w[:, cols])
            pre_up = dot(lands[r][:, :width], up_w[:, cols])
            sg = jax.nn.sigmoid(pre_gate)
            silu = pre_gate * sg
            hid_act[r, :, cols] = (silu * pre_up).astype(BF16)
            gate_act[r, :, cols] = (pre_up * sg * (1.0 + pre_gate * (1.0 - sg))).astype(BF16)
            up_act[r, :, cols] = silu.astype(BF16)
            return carry

        lax.fori_loop(0, hidden // tile, step, 0)

    def row_info(r):
        first = (experts // 128) * 128
        last = lands[r][:, width + first : width + first + 128].astype(F32)
        lane_i = lax.broadcasted_iota(jnp.int32, (rows, 128), 1)
        return [
            jnp.sum(jnp.where(lane_i == experts - first + n, last, 0.0), axis=1, keepdims=True) for n in range(4)
        ]

    def gates(r, used):
        lane = lax.broadcasted_iota(jnp.int32, (rows, experts), 1)
        mask = lands[r][:, width : width + experts].astype(F32) > 0.5
        sig = jnp.where(mask, jax.nn.sigmoid(dot_nt(lands[r][:, :width], router_ref[...])), 0.0)
        total = jnp.where(used, jnp.sum(sig, axis=1, keepdims=True), 1.0)
        share = jnp.sum(jnp.where(lane == my_expert, sig, 0.0), axis=1, keepdims=True)
        return (share / total).astype(BF16).astype(F32)

    cut = 0 if shared else 3 * width // 4

    def backward_head(r):
        if cut:

            def step(n, carry):
                cols = pl.ds(pl.multiple_of(n * tile, tile), tile)
                backs[0][:, cols] = dot_nt(lands[rounds + r][:, :cut], down_w[cols, :cut])
                return carry

            lax.fori_loop(0, hidden // tile, step, 0)

    def backward(r):
        def step(n, score):
            cols = pl.ds(pl.multiple_of(n * tile, tile), tile)
            back = dot_nt(lands[rounds + r][:, cut:], down_w[cols, cut:])
            if cut:
                back = back + backs[0][:, cols]
            gate_act[r, :, cols] = (gate_act[r, :, cols].astype(F32) * back).astype(BF16)
            up_act[r, :, cols] = (up_act[r, :, cols].astype(F32) * back).astype(BF16)
            return score + jnp.sum(hid_act[r, :, cols].astype(F32) * back, axis=1, keepdims=True)

        return lax.fori_loop(0, hidden // tile, step, jnp.zeros((rows, 1), F32))

    def own_reward(r):
        x = alls[r][mine, :width].astype(F32)
        if r > 0:
            x = (x + mixed[mine, :].astype(F32)).astype(BF16).astype(F32)
        score = jnp.sum(x * alls[rounds + r][mine, :].astype(F32), axis=1, keepdims=True) * scale
        place_t = lax.broadcasted_iota(jnp.int32, (seq, 1), 0)
        score = jnp.where(place_t < length_ref[r], score, 0.0)
        length = (jnp.zeros((1, 1), jnp.int32) + length_ref[r]).astype(F32)
        return jnp.sum(score, axis=0, keepdims=True) / length

    def vote_copies(r, phase):
        if phase == 0:
            return [
                remote(vote.at[r, 0], vote_z.at[r, k], vote_zs.at[r, 0, k], vote_zs.at[r, 1, k], peer)
                for k, peer in enumerate(exp_peers)
            ]
        return [
            remote(vote.at[r, 1], vote_s.at[r, k], vote_ss.at[r, 0, k], vote_ss.at[r, 1, k], peer)
            for k, peer in enumerate(samp_peers)
        ]

    def vote_open(r, score, gate, info, own):
        used = info[3] > 0.5
        row_score = gate * info[1] * (score * scale) / jnp.where(used, info[2], 1.0)
        lane = lax.broadcasted_iota(jnp.int32, (8, lanes), 1)
        parts = jnp.sum(jnp.where(repair_hot, row_score, 0.0), axis=0, keepdims=True)
        vote[r, 0] = jnp.where(lane == my_expert, own, 0.0) + parts
        start(vote_copies(r, 0))

    def vote_pass(r):
        total = vote[r, 0]
        for k, copy in enumerate(vote_copies(r, 0)):
            copy.wait()
            total = total + vote_z[r, k]
        vote[r, 1] = total
        start(vote_copies(r, 1))

    def vote_close(r):
        total = vote[r, 1]
        for k, copy in enumerate(vote_copies(r, 1)):
            copy.wait()
            total = total + vote_s[r, k]
        lane = lax.broadcasted_iota(jnp.int32, (8, lanes), 1).astype(F32)
        group = lane - jnp.floor((lane + 0.5) / ng) * ng
        mean = jnp.zeros((8, lanes), F32)
        for g in range(ng):
            member = (group == g) & (lane < experts)
            sums = jnp.sum(jnp.where(member, total, 0.0), axis=1, keepdims=True)
            mean = mean + jnp.where(member, sums / ns, 0.0)
        advantage = total - mean
        lane_i = lax.broadcasted_iota(jnp.int32, (8, lanes), 1)
        row = lax.broadcasted_iota(jnp.int32, (8, lanes), 0)
        adv_ref[r] = jnp.sum(jnp.where((lane_i == my_expert) & (row == 0), advantage, 0.0))
        return advantage

    def weigh(r, advantage, gate, info):
        row_adv = jnp.sum(jnp.where(repair_hot, advantage[:1, :], 0.0), axis=1, keepdims=True)
        coef = (row_adv * info[1] * gate).astype(BF16).astype(F32)
        for n, act in enumerate((gate_act, up_act, hid_act)):
            act[r] = (act[r].astype(F32) * coef).astype(BF16)
            stores(r, 2 + n).start()

    high = tokens // ns
    wide = width // ng
    tall = 4 * high
    my_yx = my_y * 2 + my_x
    my_part = my_l * 4 + my_yx

    def high_of(d):
        return pl.ds(pl.multiple_of(d * high, high), high)

    def tall_of(l):
        return pl.ds(pl.multiple_of(l * tall, tall), tall)

    def cols_of(g):
        return pl.ds(pl.multiple_of(g * wide, wide), wide)

    core_peers = [lax.rem(my_l + n, nl) for n in range(1, nl)]
    plane_peers = [lax.rem(my_yx + n, 4) for n in range(1, 4)]

    part = alls[0].at[:, :width]

    def mix_copies(phase):
        if phase == 0:
            pieces = [
                (part.at[tall_of(l), :], core_in.at[n], core_sem, n, (my_yx * nl + l, me_g))
                for n, l in enumerate(core_peers)
            ]
        elif phase == 1:
            pieces = [
                (sub.at[:, cols_of(peer[1])], cols_in.at[n], z_sem, n, peer) for n, peer in enumerate(exp_peers)
            ]
        elif phase == 2:
            pieces = [
                (half.at[high_of(p), :], rows_in.at[n], plane_sem, n, (p * nl + my_l, me_g))
                for n, p in enumerate(plane_peers)
            ]
        elif phase == 3:
            there = mixed.at[high_of(my_part), cols_of(me_g)]
            pieces = [(there, there, plane_sem, n, (p * nl + my_l, me_g)) for n, p in enumerate(plane_peers)]
        elif phase == 4:
            there = mixed.at[tall_of(my_l), cols_of(me_g)]
            pieces = [(there, there, z_sem, n, peer) for n, peer in enumerate(exp_peers)]
        else:
            there = mixed.at[tall_of(my_l), :]
            pieces = [(there, there, core_sem, n, (my_yx * nl + l, me_g)) for n, l in enumerate(core_peers)]
        late = 2 if phase > 2 else 0
        return [remote(a, b, sem.at[late, n], sem.at[late + 1, n], peer) for a, b, sem, n, peer in pieces]

    def mix_sum_core():
        finish(mix_copies(0))
        total = part[tall_of(my_l), :].astype(F32)
        for n in range(nl - 1):
            total = total + core_in[n].astype(F32)
        sub[...] = total.astype(BF16)
        start(mix_copies(1))

    def mix_sum_z():
        finish(mix_copies(1))
        total = sub[:, cols_of(me_g)].astype(F32)
        for n in range(ng - 1):
            total = total + cols_in[n].astype(F32)
        half[...] = total
        start(mix_copies(2))

    def mix_sum_plane():
        finish(mix_copies(2))
        total = half[high_of(my_yx), :]
        for n in range(3):
            total = total + rows_in[n]
        mixed[high_of(my_part), cols_of(me_g)] = total.astype(BF16)
        start(mix_copies(3))

    def step(c):
        if c < len(chunks):
            relay(c)
        scatter(c - 1)

    for c in range(1, 6):
        step(c)
    finish(loads[count:])
    for c in range(4):
        landed(c)
    stores(0, 0).start()
    project(0)
    step(6)

    info_0 = row_info(0)
    used_0 = info_0[3] > 0.5
    gate_0 = gates(0, used_0)
    slot = lax.broadcasted_iota(jnp.int32, (block, 1), 0)
    slot_group = add_all([jnp.where(slot >= g * cap, 1, 0) for g in range(1, ng)])
    choice = add_all([jnp.where(slot_group == g, chosen_ref[0, g], 0) for g in range(ng)])
    hidden_sel = jnp.zeros((block, hidden), F32)
    gate_sel = jnp.zeros((block, 1), F32)
    spot_sel = jnp.zeros((block, 1), F32)
    spot = jnp.where(used_0, info_0[0], -float(tokens))
    for d in range(ns):
        keep = choice == d
        at = slice(d * block, (d + 1) * block)
        hidden_sel = hidden_sel + jnp.where(keep, hid_act[0, at, :].astype(F32), 0.0)
        gate_sel = gate_sel + jnp.where(keep, gate_0[at], 0.0)
        spot_sel = spot_sel + jnp.where(keep, spot[at], 0.0)
    spot_sel = spot_sel + (slot_group * seq).astype(F32)
    result_ref[:block, :] = dot(hidden_sel.astype(BF16), down_w[...]).astype(BF16)
    token = lax.broadcasted_iota(jnp.int32, (block, tokens), 1).astype(F32)
    spread = jnp.where(spot_sel == token, gate_sel, 0.0)
    lead = lax.broadcasted_iota(jnp.int32, (seq, tokens), 0) + me_g * seq
    at_token = lax.broadcasted_iota(jnp.int32, (seq, tokens), 1)
    best = jnp.zeros((seq, tokens), jnp.int32) + chosen_ref[0, me_g]
    own_hot = jnp.where((lead == at_token) & (best == me_s), 1.0, 0.0)
    combine = jnp.concatenate([spread, own_hot], axis=0).astype(BF16)
    own_0 = own_reward(0)
    part[...] = dot_tn(combine, result_ref[...]).astype(BF16)
    start(mix_copies(0))
    step(7)
    mix_sum_core()
    step(8)
    step(9)
    mix_sum_z()
    step(10)
    mix_sum_plane()
    step(11)
    for c in range(4, 8):
        landed(c)
    stores(0, 1).start()
    backward_head(0)
    score_0 = backward(0)
    vote_open(0, score_0, gate_0, info_0, own_0)
    finish(mix_copies(3))
    start(mix_copies(4))
    step(12)
    step(13)
    finish(mix_copies(4))
    start(mix_copies(5))
    vote_pass(0)
    step(14)
    finish(mix_copies(5))
    for c in range(8, 12):
        landed(c)

    info_1 = row_info(1)
    used_1 = info_1[3] > 0.5
    spot_1 = jnp.where(used_1, info_1[0] + (row_group * seq).astype(F32), -1.0)
    token_r = lax.broadcasted_iota(jnp.int32, (rows, tokens), 1).astype(F32)
    lift = jnp.where(spot_1 == token_r, 1.0, 0.0).astype(BF16)
    for n in range(0, width, 2 * tile):
        cols = slice(n, n + 2 * tile)
        lifted = dot(lift, mixed[:, cols]) + lands[1][:, cols].astype(F32)
        lands[1][:, cols] = lifted.astype(BF16)
    step(15)
    stores(1, 0).start()
    project(1)
    step(16)
    gate_1 = gates(1, used_1)
    own_1 = own_reward(1)
    weigh(0, vote_close(0), gate_0, info_0)
    for c in range(12, 15):
        landed(c)
    backward_head(1)
    landed(15)
    stores(1, 1).start()
    vote_open(1, backward(1), gate_1, info_1, own_1)
    vote_pass(1)
    weigh(1, vote_close(1), gate_1, info_1)
    for r in range(rounds):
        for n in range(5):
            stores(r, n).wait()


def step_call(
    lengths, chosen, ids, base, edits, targets, router, gate_weight, up_weight, down_weight, ns, ng, block, cap
):
    rounds, top, seq = ids.shape
    experts, width = router.shape
    hidden = gate_weight.shape[1]
    extra = -(-(experts + 4) // 128) * 128
    lanes = -(-experts // 128) * 128
    rows, tokens = ns * block, ng * seq
    full = width + extra
    piece = width // 16
    chunks = []
    for r in range(rounds):
        for i in (r, rounds + r):
            for n in range(4):
                at = n * 4 * piece
                end = full if i < rounds and n == 3 else at + 4 * piece
                chunks.append((i, at, at + 2 * piece, end, piece if False else 0))
    steps = len(chunks)
    widths = [full] * rounds + [width] * rounds
    smem = pl.BlockSpec(memory_space=pltpu.SMEM)
    nl = ns // 4
    high = tokens // ns
    shared = rows * tokens > 640 * 256
    dma = pltpu.SemaphoreType.DMA
    vm = pltpu.VMEM
    return pl.pallas_call(
        functools.partial(step_kernel, ns, ng, seq, top, block, cap, rounds, extra, chunks, shared),
        out_shape=[jax.ShapeDtypeStruct((rounds * rows, width), BF16)] * 2
        + [jax.ShapeDtypeStruct((rounds * rows, hidden), BF16)] * 3
        + [jax.ShapeDtypeStruct((rounds,), F32)],
        in_specs=[smem, smem, VMEM] + [ANY] * 7,
        out_specs=[ANY] * 5 + [smem],
        scratch_shapes=[vm((rows, w), BF16) for w in widths]
        + [vm((tokens, w), BF16) for w in widths] * 2
        + [vm((rows, full), BF16)]
        + ([] if shared else [vm((rows, width), BF16), vm((rows, hidden), F32)])
        + [vm((rounds, rows, hidden), BF16)] * 3
        + [
            vm((ng, ns, rounds * seq), F32),
            vm((3, ng, ns, rounds * seq), F32),
            vm((rounds, 3, ns, tokens), F32),
            vm((rounds, 2, 2, 2 * nl * block, tokens), BF16),
            vm(router.shape, BF16),
            vm(gate_weight.shape, BF16),
            vm(up_weight.shape, BF16),
            vm(down_weight.shape, BF16),
            vm((block + seq, width), BF16),
            vm((tokens, width), BF16),
            vm((nl - 1, 4 * high, width), BF16),
            vm((4 * high, width), BF16),
            vm((3, high, width // ng), F32),
            vm((4 * high, width // ng), F32),
            vm((ng - 1, 4 * high, width // ng), BF16),
            vm((rounds, 2, 8, lanes), F32),
            vm((rounds, ng - 1, 8, lanes), F32),
            vm((rounds, ns - 1, 8, lanes), F32),
            dma((2 * rounds + 5,)),
            dma((rounds, 5)),
            dma((2, ng - 1)),
            dma((2, 2)),
            dma((2, steps, ng - 1)),
            dma((2, steps, ng - 1)),
            dma((2, steps)),
            dma((steps, 2)),
            dma((steps, 2)),
            dma((steps, 2)),
            dma((steps, 2)),
            dma((steps, 2, 2 * nl, 2)),
            dma((steps, 2, 2 * nl, 2)),
            dma((4, nl - 1)),
            dma((4, 3)),
            dma((4, ng - 1)),
            dma((rounds, 2, ng - 1)),
            dma((rounds, 2, ns - 1)),
        ],
        compiler_params=pltpu.CompilerParams(
            collective_id=0, has_side_effects=True, vmem_limit_bytes=63 * 2**20
        ),
    )(lengths, chosen, ids, base, edits, targets, router, gate_weight, up_weight, down_weight)


def per_device(
    prompt_states, edit_offsets, targets, router, route_ids, chosen, lengths, w_gate, w_up, w_down
):
    seq = prompt_states.shape[2]
    rounds = route_ids.shape[0]
    top = route_ids.shape[4]
    experts = router.shape[1]
    cap = seq * top * 5 // (4 * experts)
    samplers = lax.axis_size("samp")
    groups = lax.axis_size("exp")
    block = -(-groups * cap // 16) * 16
    x, target, gate_side, up_side, weighted, advantage = step_call(
        lengths.reshape(rounds),
        chosen,
        route_ids[:, 0, 0].swapaxes(1, 2),
        prompt_states[0, 0],
        edit_offsets[:, 0, 0],
        targets[:, 0, 0],
        router.T,
        w_gate[0],
        w_up[0],
        w_down[0],
        samplers,
        groups,
        block,
        cap,
    )
    return (
        dot_tn(x, gate_side).astype(BF16)[None],
        dot_tn(x, up_side).astype(BF16)[None],
        dot_tn(weighted, target).astype(BF16)[None],
        advantage.reshape(rounds, 1, 1),
    )


def solution(mesh):
    placed = (
        P("exp", "samp", None, None),
        P(None, "exp", "samp", None, None),
        P(None, "exp", "samp", None, None),
        P(),
        P(None, "exp", "samp", None, None),
        P(),
        P(None, "exp", "samp"),
        P(("samp", "exp"), None, None),
        P(("samp", "exp"), None, None),
        P(("samp", "exp"), None, None),
    )
    return jax.shard_map(
        per_device,
        mesh=mesh,
        in_specs=placed,
        out_specs=(
            P(("samp", "exp"), None, None),
            P(("samp", "exp"), None, None),
            P(("samp", "exp"), None, None),
            P(None, "exp", "samp"),
        ),
        check_vma=False,
    )
```

```python
import functools
import math

import jax
import jax.numpy as jnp
from jax import lax
from jax.experimental import pallas as pl
from jax.experimental.pallas import tpu as pltpu
from jax.sharding import PartitionSpec as P

F32 = jnp.float32
BF16 = jnp.bfloat16


def dot(a, b):
    return jnp.dot(a, b, preferred_element_type=F32)


def dot_tn(a, b):
    return lax.dot_general(a, b, (((0,), (0,)), ((), ())), preferred_element_type=F32)


def dot_nt(a, b):
    return lax.dot_general(a, b, (((1,), (1,)), ((), ())), preferred_element_type=F32)


MESH = pl.DeviceIdType.MESH
VMEM = pl.BlockSpec(memory_space=pltpu.VMEM)
ANY = pl.BlockSpec(memory_space=pl.ANY)


def greet(peers):
    for peer in peers:
        pl.semaphore_signal(pltpu.get_barrier_semaphore(), inc=1, device_id=peer, device_id_type=MESH)


def remote(src, dst, send, recv, peer):
    return pltpu.make_async_remote_copy(
        src_ref=src, dst_ref=dst, send_sem=send, recv_sem=recv, device_id=peer, device_id_type=MESH
    )


def add_all(terms):
    total = terms[0]
    for term in terms[1:]:
        total = total + term
    return total


def step_kernel(ns, ng, seq, top, block, cap, rounds, extra, chunks, shared, *refs):
    count = 2 * rounds
    length_ref, chosen_ref, ids_ref = refs[:3]
    base_hbm, edit_hbm, target_hbm, router_hbm, gate_hbm, up_hbm, down_hbm = refs[3:10]
    outs, adv_ref = refs[10:15], refs[15]
    rest = list(refs[16:])

    def take(n):
        taken = rest[:n]
        del rest[:n]
        return taken

    lands, alls, pairs, sends = take(count), take(count), take(count), take(1 if shared else 2)
    backs = take(0 if shared else 1)
    (
        gate_act, up_act, hid_act, code, codes, lines, place, router_ref, gate_w, up_w, down_w, result_ref, mixed,
        core_in, sub, rows_in, half, cols_in, vote, vote_z, vote_s, load_sem, store_sem, code_sem, line_sem,
        gs, gr, fs, bs, br, rs, rr, ss, sr, core_sem, plane_sem, z_sem, vote_zs, vote_ss,
    ) = rest
    width = base_hbm.shape[1]
    hidden = gate_w.shape[1]
    experts = ns * ng
    tokens = ng * seq
    rows = ns * block
    nl = ns // 4
    fan = 2 * nl
    tile = 256
    lanes = vote.shape[-1]
    me_s, me_g = lax.axis_index("samp"), lax.axis_index("exp")
    my_y, my_x, my_l = me_s // fan, lax.rem(me_s // nl, 2), lax.rem(me_s, nl)
    my_expert = me_s * ng + me_g

    def samp_at(y, x, l):
        return (y * 2 + x) * nl + l

    partners = [samp_at(1 - my_y, my_x, my_l), samp_at(my_y, 1 - my_x, my_l)]
    exp_peers = [(me_s, lax.rem(me_g + k, ng)) for k in range(1, ng)]
    samp_peers = [(lax.rem(me_s + k, ns), me_g) for k in range(1, ns)]
    mine = pl.ds(pl.multiple_of(me_g * seq, seq), seq)
    greet(exp_peers + samp_peers)

    def rows_of(d):
        return pl.ds(pl.multiple_of(d * block, block), block)

    loads = [
        pltpu.make_async_copy(source, target, load_sem.at[n])
        for n, (source, target) in enumerate(
            [(base_hbm, alls[0].at[mine, :width])]
            + [(target_hbm.at[0], alls[rounds].at[mine, :])]
            + [(edit_hbm.at[r - 1], alls[r].at[mine, :width]) for r in range(1, rounds)]
            + [(target_hbm.at[r], alls[rounds + r].at[mine, :]) for r in range(1, rounds)]
            + [(base_hbm, result_ref.at[block:, :])]
            + [(router_hbm, router_ref), (gate_hbm, gate_w), (up_hbm, up_w), (down_hbm, down_w)]
        )
    ]
    order = [0, rounds] + list(range(1, rounds)) + list(range(rounds + 1, count))
    for copy in loads:
        copy.start()

    row_p = lax.broadcasted_iota(jnp.int32, (experts, seq), 0).astype(F32)
    block_p = jnp.floor((row_p + 0.5) / ns)
    order_p = (row_p - block_p * ns) * ng + block_p
    row_m = lax.broadcasted_iota(jnp.int32, (extra, seq), 0)
    position = lax.broadcasted_iota(jnp.int32, (extra, seq), 1)
    row_e = lax.broadcasted_iota(jnp.int32, (seq, seq), 0)
    col_e = lax.broadcasted_iota(jnp.int32, (seq, seq), 1)
    eye = jnp.where(row_e == col_e, 1.0, 0.0).astype(BF16)
    upto = jnp.where(row_e <= col_e, 1.0, 0.0).astype(BF16)
    codes_own = []
    for r in range(rounds):
        ids = ids_ref[r]
        ids_f = ids.astype(F32)
        hit = add_all([jnp.where(ids_f[k : k + 1, :] == order_p, 1.0, 0.0) for k in range(top)])
        rank = dot(hit.astype(BF16), upto) - 1.0
        offset = (jnp.zeros((experts, seq), jnp.int32) + me_g * cap).astype(F32)
        codes_own.append(jnp.where(hit > 0.5, rank + offset, -1.0))
        length = jnp.zeros((extra, seq), jnp.int32) + length_ref[r]
        info = jnp.where(row_m == experts, position, 0)
        info = info + jnp.where((row_m == experts + 1) & (position < length), 1, 0)
        info = info + jnp.where(row_m == experts + 2, length, 0)
        info = info + jnp.where(row_m == experts + 3, 1, 0)
        for k in range(top):
            info = info + jnp.where(ids[k : k + 1, :] == row_m, 1, 0)
        alls[r][mine, width:] = dot_nt(eye, info.astype(F32).astype(BF16)).astype(BF16)
    line = jnp.concatenate(codes_own, axis=1)
    for g in range(ng):
        code[g] = line[g * ns : (g + 1) * ns, :]
    codes[0, me_g] = code[me_g]
    pl.semaphore_wait(pltpu.get_barrier_semaphore(), len(exp_peers + samp_peers))


    def z_piece(c, kind):
        i, lo, mid, hi, quota = chunks[c]
        return (alls[i], lo, hi) if kind == 0 else (pairs[i], mid - quota, mid + quota)

    def gather_copies(c, kind):
        tokens_ref, a, b = z_piece(c, kind)
        own = tokens_ref.at[mine, a:b]
        return [remote(own, own, gs.at[kind, c, k], gr.at[kind, c, k], p) for k, p in enumerate(exp_peers)]

    def ahead_copies(c):
        i, lo, mid, hi, quota = chunks[c]
        cuts = [(mid - quota, mid), (mid, mid + quota)] if quota else []
        return [
            remote(alls[i].at[mine, a:b], pairs[i].at[mine, a:b], bs.at[c, h], br.at[c, h], (partners[h], me_g))
            for h, (a, b) in enumerate(cuts)
        ]

    def relay_copies(c):
        i, lo, mid, hi, quota = chunks[c]
        return [
            remote(alls[i].at[:, a:b], pairs[i].at[:, a:b], rs.at[c, h], rr.at[c, h], (partners[h], me_g))
            for h, (a, b) in enumerate([(lo, mid - quota), (mid + quota, hi)])
            if a < b
        ]

    def start(copies):
        for copy in copies:
            copy.start()
        return copies

    def finish(copies):
        for copy in copies:
            copy.wait()

    ready = set()
    chain = ng == 4

    def z_start(c, kind):
        copies = gather_copies(c, kind)
        if chain:
            copies[1].start()
            pl.when(me_g != ng - 1)(copies[0].start)
            pl.when(me_g != 0)(copies[2].start)
        else:
            start(copies)

    def forward_copy(c, kind, owner, there):
        tokens_ref, a, b = z_piece(c, kind)
        piece = tokens_ref.at[owner * seq : (owner + 1) * seq, a:b]
        return remote(piece, piece, fs.at[kind, c], gr.at[kind, c, (there - owner) % ng - 1], (me_s, there))

    def z_forward(c, kind):
        if chain:
            gather_copies(c, kind)[1].wait_recv()
            pl.when(me_g == 1)(forward_copy(c, kind, 3, 0).start)
            pl.when(me_g == 2)(forward_copy(c, kind, 0, 3).start)

    def z_finish(c, kind):
        copies = gather_copies(c, kind)
        if chain:
            copies[1].wait_send()
            copies[0].wait_recv()
            copies[2].wait_recv()
            pl.when(me_g != ng - 1)(copies[0].wait_send)
            pl.when(me_g != 0)(copies[2].wait_send)
            pl.when((me_g == 1) | (me_g == 2))(forward_copy(c, kind, 0, 3).wait_send)
        else:
            finish(copies)

    def gather(c):
        if c < len(chunks):
            i = chunks[c][0]
            if i not in ready:
                ready.add(i)
                loads[order.index(i)].wait()
            start(ahead_copies(c))
            z_start(c, 0)

    def forward(c):
        if c < len(chunks):
            z_forward(c, 0)
            if chunks[c][4]:
                finish(ahead_copies(c))
                z_start(c, 1)

    def relay(c):
        z_finish(c, 0)
        start(relay_copies(c))
        gather(c + 2)

    def dest_of(h, k):
        l = lax.rem(my_l + lax.rem(k, nl), nl)
        if h == 0:
            return samp_at(my_y, lax.rem(my_x + k // nl, 2), l)
        return samp_at(lax.rem(my_y + k // nl, 2), my_x, l)

    def cols_at(c, h):
        i, lo, mid, hi, quota = chunks[c]
        return (lo, mid) if h == 0 else (mid, hi)

    def buffer_of(c):
        return sends[0 if shared else chunks[c][0] // rounds]

    def slot_copy(c, h, k, b):
        i = chunks[c][0]
        a, e = cols_at(c, h)
        home = me_s if b == 0 else partners[h]
        return remote(
            buffer_of(c).at[rows_of(b * fan + k), a:e],
            lands[i].at[rows_of(home), a:e],
            ss.at[c, h, k, b],
            sr.at[c, h, k, b],
            (dest_of(h, k), me_g),
        )

    done = set()

    def landed(c):
        if c in done:
            return
        done.add(c)

        def step(k, carry):
            for h in range(2):
                for b in range(2):
                    slot_copy(c, h, k, b).wait()
            return carry

        lax.fori_loop(1, fan, step, 0)

    def scatter(c):
        i = chunks[c][0]
        finish(relay_copies(c))
        if chunks[c][4]:
            z_finish(c, 1)
        for p in range(c):
            if (shared or chunks[p][0] // rounds == i // rounds) and chunks[p][1] == chunks[c][1]:
                landed(p)
        for h in range(2):
            a, e = cols_at(c, h)
            for b in range(2):
                tokens_ref = alls[i] if b == 0 else pairs[i]
                placed = dot(place[i % rounds, h, b], tokens_ref[:, a:e]).astype(BF16)
                buffer_of(c)[(b * fan + 1) * block : (b + 1) * fan * block, a:e] = placed[block:]
                home = me_s if b == 0 else partners[h]
                lands[i][rows_of(home), a:e] = placed[:block]

                def step(n, carry, h=h, b=b):
                    slot_copy(c, h, fan - n, b).start()
                    return carry

                lax.fori_loop(1, fan, step, 0)

    code_copies = start(
        [
            remote(code.at[peer[1]], codes.at[0, me_g], code_sem.at[0, k], code_sem.at[1, k], peer)
            for k, peer in enumerate(exp_peers)
        ]
    )
    gather(0)
    gather(1)
    finish(code_copies)
    line_copies = start(
        [
            remote(codes.at[0], codes.at[1 + h], line_sem.at[0, h], line_sem.at[1, h], (partners[h], me_g))
            for h in range(2)
        ]
    )
    forward(0)
    relay(0)
    forward(1)
    finish(line_copies)
    slots = lax.broadcasted_iota(jnp.int32, (block, tokens), 0).astype(F32)

    def build_places(r):
        for who in range(3):
            lines[r, who] = jnp.concatenate(
                [codes[who, g][:, r * seq : (r + 1) * seq] for g in range(ng)], axis=1
            )
        for h in range(2):
            for b in range(2):
                for k in range(fan):
                    line = lines[r, 0 if b == 0 else 1 + h, pl.ds(dest_of(h, k), 1), :]
                    hit = jnp.where(line == slots, 1.0, 0.0)
                    place[r, h, b, k * block : (k + 1) * block, :] = hit.astype(BF16)

    build_places(0)

    row_i = lax.broadcasted_iota(jnp.int32, (rows, 1), 0)
    row_samp = add_all([jnp.where(row_i >= d * block, 1, 0) for d in range(1, ns)])
    row_slot = row_i - row_samp * block
    row_group = add_all([jnp.where(row_slot >= g * cap, 1, 0) for g in range(1, ng)])
    lane_v = lax.broadcasted_iota(jnp.int32, (rows, lanes), 1)
    repair_hot = row_samp * ng + row_group == lane_v
    scale = 1.0 / math.sqrt(width)

    def stores(r, n):
        source = (lands[r].at[:, :width], lands[rounds + r], gate_act.at[r], up_act.at[r], hid_act.at[r])[n]
        target = outs[n].at[r * rows : (r + 1) * rows, :]
        return pltpu.make_async_copy(source, target, store_sem.at[r, n])

    def project(r):
        def step(n, carry):
            cols = pl.ds(pl.multiple_of(n * tile, tile), tile)
            pre_gate = dot(lands[r][:, :width], gate_w[:, cols])
            pre_up = dot(lands[r][:, :width], up_w[:, cols])
            sg = jax.nn.sigmoid(pre_gate)
            silu = pre_gate * sg
            hid_act[r, :, cols] = (silu * pre_up).astype(BF16)
            gate_act[r, :, cols] = (pre_up * sg * (1.0 + pre_gate * (1.0 - sg))).astype(BF16)
            up_act[r, :, cols] = silu.astype(BF16)
            return carry

        lax.fori_loop(0, hidden // tile, step, 0)

    def row_info(r):
        first = (experts // 128) * 128
        last = lands[r][:, width + first : width + first + 128].astype(F32)
        lane_i = lax.broadcasted_iota(jnp.int32, (rows, 128), 1)
        return [
            jnp.sum(jnp.where(lane_i == experts - first + n, last, 0.0), axis=1, keepdims=True) for n in range(4)
        ]

    def gates(r, used):
        lane = lax.broadcasted_iota(jnp.int32, (rows, experts), 1)
        mask = lands[r][:, width : width + experts].astype(F32) > 0.5
        sig = jnp.where(mask, jax.nn.sigmoid(dot_nt(lands[r][:, :width], router_ref[...])), 0.0)
        total = jnp.where(used, jnp.sum(sig, axis=1, keepdims=True), 1.0)
        share = jnp.sum(jnp.where(lane == my_expert, sig, 0.0), axis=1, keepdims=True)
        return (share / total).astype(BF16).astype(F32)

    cut = 0 if shared else 3 * width // 4

    def backward_head(r):
        if cut:

            def step(n, carry):
                cols = pl.ds(pl.multiple_of(n * tile, tile), tile)
                backs[0][:, cols] = dot_nt(lands[rounds + r][:, :cut], down_w[cols, :cut])
                return carry

            lax.fori_loop(0, hidden // tile, step, 0)

    def backward(r):
        def step(n, score):
            cols = pl.ds(pl.multiple_of(n * tile, tile), tile)
            back = dot_nt(lands[rounds + r][:, cut:], down_w[cols, cut:])
            if cut:
                back = back + backs[0][:, cols]
            gate_act[r, :, cols] = (gate_act[r, :, cols].astype(F32) * back).astype(BF16)
            up_act[r, :, cols] = (up_act[r, :, cols].astype(F32) * back).astype(BF16)
            return score + jnp.sum(hid_act[r, :, cols].astype(F32) * back, axis=1, keepdims=True)

        return lax.fori_loop(0, hidden // tile, step, jnp.zeros((rows, 1), F32))

    def own_reward(r):
        x = alls[r][mine, :width].astype(F32)
        if r > 0:
            x = (x + mixed[mine, :].astype(F32)).astype(BF16).astype(F32)
        score = jnp.sum(x * alls[rounds + r][mine, :].astype(F32), axis=1, keepdims=True) * scale
        place_t = lax.broadcasted_iota(jnp.int32, (seq, 1), 0)
        score = jnp.where(place_t < length_ref[r], score, 0.0)
        length = (jnp.zeros((1, 1), jnp.int32) + length_ref[r]).astype(F32)
        return jnp.sum(score, axis=0, keepdims=True) / length

    def vote_copies(r, phase):
        if phase == 0:
            return [
                remote(vote.at[r, 0], vote_z.at[r, k], vote_zs.at[r, 0, k], vote_zs.at[r, 1, k], peer)
                for k, peer in enumerate(exp_peers)
            ]
        return [
            remote(vote.at[r, 1], vote_s.at[r, k], vote_ss.at[r, 0, k], vote_ss.at[r, 1, k], peer)
            for k, peer in enumerate(samp_peers)
        ]

    def vote_open(r, score, gate, info, own):
        used = info[3] > 0.5
        row_score = gate * info[1] * (score * scale) / jnp.where(used, info[2], 1.0)
        lane = lax.broadcasted_iota(jnp.int32, (8, lanes), 1)
        parts = jnp.sum(jnp.where(repair_hot, row_score, 0.0), axis=0, keepdims=True)
        vote[r, 0] = jnp.where(lane == my_expert, own, 0.0) + parts
        start(vote_copies(r, 0))

    def vote_pass(r):
        total = vote[r, 0]
        for k, copy in enumerate(vote_copies(r, 0)):
            copy.wait()
            total = total + vote_z[r, k]
        vote[r, 1] = total
        start(vote_copies(r, 1))

    def vote_close(r):
        total = vote[r, 1]
        for k, copy in enumerate(vote_copies(r, 1)):
            copy.wait()
            total = total + vote_s[r, k]
        lane = lax.broadcasted_iota(jnp.int32, (8, lanes), 1).astype(F32)
        group = lane - jnp.floor((lane + 0.5) / ng) * ng
        mean = jnp.zeros((8, lanes), F32)
        for g in range(ng):
            member = (group == g) & (lane < experts)
            sums = jnp.sum(jnp.where(member, total, 0.0), axis=1, keepdims=True)
            mean = mean + jnp.where(member, sums / ns, 0.0)
        advantage = total - mean
        lane_i = lax.broadcasted_iota(jnp.int32, (8, lanes), 1)
        row = lax.broadcasted_iota(jnp.int32, (8, lanes), 0)
        adv_ref[r] = jnp.sum(jnp.where((lane_i == my_expert) & (row == 0), advantage, 0.0))
        return advantage

    def weigh(r, advantage, gate, info):
        row_adv = jnp.sum(jnp.where(repair_hot, advantage[:1, :], 0.0), axis=1, keepdims=True)
        coef = (row_adv * info[1] * gate).astype(BF16).astype(F32)
        for n, act in enumerate((gate_act, up_act, hid_act)):
            act[r] = (act[r].astype(F32) * coef).astype(BF16)
            stores(r, 2 + n).start()

    high = tokens // ns
    wide = width // ng
    tall = 4 * high
    my_yx = my_y * 2 + my_x
    my_part = my_l * 4 + my_yx

    def high_of(d):
        return pl.ds(pl.multiple_of(d * high, high), high)

    def tall_of(l):
        return pl.ds(pl.multiple_of(l * tall, tall), tall)

    def cols_of(g):
        return pl.ds(pl.multiple_of(g * wide, wide), wide)

    core_peers = [lax.rem(my_l + n, nl) for n in range(1, nl)]
    plane_peers = [lax.rem(my_yx + n, 4) for n in range(1, 4)]

    part = alls[0].at[:, :width]

    def mix_copies(phase):
        if phase == 0:
            pieces = [
                (part.at[tall_of(l), :], core_in.at[n], core_sem, n, (my_yx * nl + l, me_g))
                for n, l in enumerate(core_peers)
            ]
        elif phase == 1:
            pieces = [
                (sub.at[:, cols_of(peer[1])], cols_in.at[n], z_sem, n, peer) for n, peer in enumerate(exp_peers)
            ]
        elif phase == 2:
            pieces = [
                (half.at[high_of(p), :], rows_in.at[n], plane_sem, n, (p * nl + my_l, me_g))
                for n, p in enumerate(plane_peers)
            ]
        elif phase == 3:
            there = mixed.at[high_of(my_part), cols_of(me_g)]
            pieces = [(there, there, plane_sem, n, (p * nl + my_l, me_g)) for n, p in enumerate(plane_peers)]
        elif phase == 4:
            there = mixed.at[tall_of(my_l), cols_of(me_g)]
            pieces = [(there, there, z_sem, n, peer) for n, peer in enumerate(exp_peers)]
        else:
            there = mixed.at[tall_of(my_l), :]
            pieces = [(there, there, core_sem, n, (my_yx * nl + l, me_g)) for n, l in enumerate(core_peers)]
        late = 2 if phase > 2 else 0
        return [remote(a, b, sem.at[late, n], sem.at[late + 1, n], peer) for a, b, sem, n, peer in pieces]

    def mix_sum_core():
        finish(mix_copies(0))
        total = part[tall_of(my_l), :].astype(F32)
        for n in range(nl - 1):
            total = total + core_in[n].astype(F32)
        sub[...] = total.astype(BF16)
        start(mix_copies(1))

    def mix_sum_z():
        finish(mix_copies(1))
        total = sub[:, cols_of(me_g)].astype(F32)
        for n in range(ng - 1):
            total = total + cols_in[n].astype(F32)
        half[...] = total
        start(mix_copies(2))

    def mix_sum_plane():
        finish(mix_copies(2))
        total = half[high_of(my_yx), :]
        for n in range(3):
            total = total + rows_in[n]
        mixed[high_of(my_part), cols_of(me_g)] = total.astype(BF16)
        start(mix_copies(3))

    def step(c):
        if c < len(chunks):
            relay(c)
        scatter(c - 1)
        forward(c + 1)

    for c in range(1, 6):
        step(c)
    for r in range(1, rounds):
        build_places(r)
    finish(loads[count:])
    for c in range(4):
        landed(c)
    stores(0, 0).start()
    project(0)
    step(6)

    info_0 = row_info(0)
    used_0 = info_0[3] > 0.5
    gate_0 = gates(0, used_0)
    slot = lax.broadcasted_iota(jnp.int32, (block, 1), 0)
    slot_group = add_all([jnp.where(slot >= g * cap, 1, 0) for g in range(1, ng)])
    choice = add_all([jnp.where(slot_group == g, chosen_ref[0, g], 0) for g in range(ng)])
    hidden_sel = jnp.zeros((block, hidden), F32)
    gate_sel = jnp.zeros((block, 1), F32)
    spot_sel = jnp.zeros((block, 1), F32)
    spot = jnp.where(used_0, info_0[0], -float(tokens))
    for d in range(ns):
        keep = choice == d
        at = slice(d * block, (d + 1) * block)
        hidden_sel = hidden_sel + jnp.where(keep, hid_act[0, at, :].astype(F32), 0.0)
        gate_sel = gate_sel + jnp.where(keep, gate_0[at], 0.0)
        spot_sel = spot_sel + jnp.where(keep, spot[at], 0.0)
    spot_sel = spot_sel + (slot_group * seq).astype(F32)
    result_ref[:block, :] = dot(hidden_sel.astype(BF16), down_w[...]).astype(BF16)
    token = lax.broadcasted_iota(jnp.int32, (block, tokens), 1).astype(F32)
    spread = jnp.where(spot_sel == token, gate_sel, 0.0)
    lead = lax.broadcasted_iota(jnp.int32, (seq, tokens), 0) + me_g * seq
    at_token = lax.broadcasted_iota(jnp.int32, (seq, tokens), 1)
    best = jnp.zeros((seq, tokens), jnp.int32) + chosen_ref[0, me_g]
    own_hot = jnp.where((lead == at_token) & (best == me_s), 1.0, 0.0)
    combine = jnp.concatenate([spread, own_hot], axis=0).astype(BF16)
    own_0 = own_reward(0)
    part[...] = dot_tn(combine, result_ref[...]).astype(BF16)
    start(mix_copies(0))
    step(7)
    mix_sum_core()
    step(8)
    step(9)
    mix_sum_z()
    step(10)
    mix_sum_plane()
    step(11)
    for c in range(4, 8):
        landed(c)
    stores(0, 1).start()
    backward_head(0)
    score_0 = backward(0)
    vote_open(0, score_0, gate_0, info_0, own_0)
    finish(mix_copies(3))
    start(mix_copies(4))
    step(12)
    step(13)
    finish(mix_copies(4))
    start(mix_copies(5))
    vote_pass(0)
    step(14)
    finish(mix_copies(5))
    for c in range(8, 12):
        landed(c)

    info_1 = row_info(1)
    used_1 = info_1[3] > 0.5
    spot_1 = jnp.where(used_1, info_1[0] + (row_group * seq).astype(F32), -1.0)
    token_r = lax.broadcasted_iota(jnp.int32, (rows, tokens), 1).astype(F32)
    lift = jnp.where(spot_1 == token_r, 1.0, 0.0).astype(BF16)
    for n in range(0, width, 2 * tile):
        cols = slice(n, n + 2 * tile)
        lifted = dot(lift, mixed[:, cols]) + lands[1][:, cols].astype(F32)
        lands[1][:, cols] = lifted.astype(BF16)
    step(15)
    stores(1, 0).start()
    project(1)
    step(16)
    gate_1 = gates(1, used_1)
    own_1 = own_reward(1)
    weigh(0, vote_close(0), gate_0, info_0)
    for c in range(12, 15):
        landed(c)
    backward_head(1)
    landed(15)
    stores(1, 1).start()
    vote_open(1, backward(1), gate_1, info_1, own_1)
    vote_pass(1)
    weigh(1, vote_close(1), gate_1, info_1)
    for r in range(rounds):
        for n in range(5):
            stores(r, n).wait()


def step_call(
    lengths, chosen, ids, base, edits, targets, router, gate_weight, up_weight, down_weight, ns, ng, block, cap
):
    rounds, top, seq = ids.shape
    experts, width = router.shape
    hidden = gate_weight.shape[1]
    extra = -(-(experts + 4) // 128) * 128
    lanes = -(-experts // 128) * 128
    rows, tokens = ns * block, ng * seq
    full = width + extra
    piece = width // 16
    chunks = []
    for r in range(rounds):
        for i in (r, rounds + r):
            for n in range(4):
                at = n * 4 * piece
                end = full if i < rounds and n == 3 else at + 4 * piece
                chunks.append((i, at, at + 2 * piece, end, piece if False else 0))
    steps = len(chunks)
    widths = [full] * rounds + [width] * rounds
    smem = pl.BlockSpec(memory_space=pltpu.SMEM)
    nl = ns // 4
    high = tokens // ns
    shared = rows * tokens > 640 * 256
    dma = pltpu.SemaphoreType.DMA
    vm = pltpu.VMEM
    return pl.pallas_call(
        functools.partial(step_kernel, ns, ng, seq, top, block, cap, rounds, extra, chunks, shared),
        out_shape=[jax.ShapeDtypeStruct((rounds * rows, width), BF16)] * 2
        + [jax.ShapeDtypeStruct((rounds * rows, hidden), BF16)] * 3
        + [jax.ShapeDtypeStruct((rounds,), F32)],
        in_specs=[smem, smem, VMEM] + [ANY] * 7,
        out_specs=[ANY] * 5 + [smem],
        scratch_shapes=[vm((rows, w), BF16) for w in widths]
        + [vm((tokens, w), BF16) for w in widths] * 2
        + [vm((rows, full), BF16)]
        + ([] if shared else [vm((rows, width), BF16), vm((rows, hidden), F32)])
        + [vm((rounds, rows, hidden), BF16)] * 3
        + [
            vm((ng, ns, rounds * seq), F32),
            vm((3, ng, ns, rounds * seq), F32),
            vm((rounds, 3, ns, tokens), F32),
            vm((rounds, 2, 2, 2 * nl * block, tokens), BF16),
            vm(router.shape, BF16),
            vm(gate_weight.shape, BF16),
            vm(up_weight.shape, BF16),
            vm(down_weight.shape, BF16),
            vm((block + seq, width), BF16),
            vm((tokens, width), BF16),
            vm((nl - 1, 4 * high, width), BF16),
            vm((4 * high, width), BF16),
            vm((3, high, width // ng), F32),
            vm((4 * high, width // ng), F32),
            vm((ng - 1, 4 * high, width // ng), BF16),
            vm((rounds, 2, 8, lanes), F32),
            vm((rounds, ng - 1, 8, lanes), F32),
            vm((rounds, ns - 1, 8, lanes), F32),
            dma((2 * rounds + 5,)),
            dma((rounds, 5)),
            dma((2, ng - 1)),
            dma((2, 2)),
            dma((2, steps, ng - 1)),
            dma((2, steps, ng - 1)),
            dma((2, steps)),
            dma((steps, 2)),
            dma((steps, 2)),
            dma((steps, 2)),
            dma((steps, 2)),
            dma((steps, 2, 2 * nl, 2)),
            dma((steps, 2, 2 * nl, 2)),
            dma((4, nl - 1)),
            dma((4, 3)),
            dma((4, ng - 1)),
            dma((rounds, 2, ng - 1)),
            dma((rounds, 2, ns - 1)),
        ],
        compiler_params=pltpu.CompilerParams(
            collective_id=0, has_side_effects=True, vmem_limit_bytes=63 * 2**20
        ),
    )(lengths, chosen, ids, base, edits, targets, router, gate_weight, up_weight, down_weight)


def per_device(
    prompt_states, edit_offsets, targets, router, route_ids, chosen, lengths, w_gate, w_up, w_down
):
    seq = prompt_states.shape[2]
    rounds = route_ids.shape[0]
    top = route_ids.shape[4]
    experts = router.shape[1]
    cap = seq * top * 5 // (4 * experts)
    samplers = lax.axis_size("samp")
    groups = lax.axis_size("exp")
    block = -(-groups * cap // 16) * 16
    x, target, gate_side, up_side, weighted, advantage = step_call(
        lengths.reshape(rounds),
        chosen,
        route_ids[:, 0, 0].swapaxes(1, 2),
        prompt_states[0, 0],
        edit_offsets[:, 0, 0],
        targets[:, 0, 0],
        router.T,
        w_gate[0],
        w_up[0],
        w_down[0],
        samplers,
        groups,
        block,
        cap,
    )
    return (
        dot_tn(x, gate_side).astype(BF16)[None],
        dot_tn(x, up_side).astype(BF16)[None],
        dot_tn(weighted, target).astype(BF16)[None],
        advantage.reshape(rounds, 1, 1),
    )


def solution(mesh):
    placed = (
        P("exp", "samp", None, None),
        P(None, "exp", "samp", None, None),
        P(None, "exp", "samp", None, None),
        P(),
        P(None, "exp", "samp", None, None),
        P(),
        P(None, "exp", "samp"),
        P(("samp", "exp"), None, None),
        P(("samp", "exp"), None, None),
        P(("samp", "exp"), None, None),
    )
    return jax.shard_map(
        per_device,
        mesh=mesh,
        in_specs=placed,
        out_specs=(
            P(("samp", "exp"), None, None),
            P(("samp", "exp"), None, None),
            P(("samp", "exp"), None, None),
            P(None, "exp", "samp"),
        ),
        check_vma=False,
    )
```
